512 devices in a mesh: expert: 32 (over y, z_hi, core), tensor: 4 (over x), dp: 4 (over z_lo).
Axes of the slice: x: 4, y: 8, z: 8 (z_hi: 2, z_lo: 4; z = z_hi * 4 + z_lo), core: 2. Of those that a mesh axis runs over, the one named last changes fastest.
Arguments:
- tokens: bfloat16 [16384, 4096], P(('expert', 'dp'), 'tensor'), may hold values from -6 to 6
- routes: int32 [16384, 2], P(('expert', 'dp')), may hold values from 0 to 31, all different within a row; in each aligned block of 128 rows (0 to 127, 128 to 255, ...) at most 10 rows name the same one
- gate_prob: float32 [16384, 2], P(('expert', 'dp')), may hold values from 0.05 to 1
- token_count: int32 [128], P(('expert', 'dp')), may hold values from 1 to 128, 12288 in all
- gate_weight: bfloat16 [32, 4096, 1536], P(None, ('expert', 'dp'), 'tensor'), may hold values from -0.09375 to 0.09375
- up_weight: bfloat16 [32, 4096, 1536], P(None, ('expert', 'dp'), 'tensor'), may hold values from -0.09375 to 0.09375
- down_weight: bfloat16 [32, 4096, 1536], P(None, ('expert', 'dp'), 'tensor'), may hold values from -0.15625 to 0.15625
Outputs:
- mixed: bfloat16 [16384, 4096], P(('expert', 'dp'), 'tensor')
The draws below stay inside these ranges and needn't reach their ends.
Inputs may be any that keep to these rules, and one draw needn't show every extreme that they name: `routes`: each row names 2 different experts; among the rows of one group (aligned blocks of 128 rows) no expert is named by more than 10 rows. `token_count`: rows of a group at or past its count are padding.
All inputs are finite; a program needn't handle non-finite values.
Results may differ from the reference program's by a relative error of at most 0.012.
Values may be sent and summed in bfloat16 or wider, within the bound.
A program may use at most 64 MiB of HBM per device.

```python
import math
import jax
import jax.numpy as jnp
import numpy as np
from jax import lax

D = 4096
FF = 1536
TOPW = 2
TOK_DEV = 128
EXPERTS = 32
GROUPS = 128
TOKENS = 16384
CAP = 10
N_TENSOR = 4


def shard_levels(rng, extent, pieces, smallest, largest):
    def one(dim, shards_of):
        heights = jax.random.uniform(jax.random.fold_in(jax.random.fold_in(rng, 6), dim), (shards_of,), jnp.float32, smallest / len(pieces), largest / len(pieces))
        return jnp.repeat(jnp.exp(heights), extent[dim] // shards_of).reshape((-1,) + (1,) * (len(extent) - dim - 1))

    level = one(*pieces[0])
    for cut in pieces[1:]:
        level = level * one(*cut)
    return level


def split_up(count, total, most, lean):
    portions = [(1 << 20) // math.isqrt(standing ** lean) + 1 for standing in range(2, count + 1)]
    surplus, counts = total - most - (count - 1), [1] * (count - 1)
    while surplus > 0:
        movable = [i for i in range(count - 1) if counts[i] < most]
        whole, budget = sum([portions[i] for i in movable]), surplus
        for i in movable:
            extra = min(most - counts[i], max(1, budget * portions[i] // whole), surplus)
            counts[i] = counts[i] + extra
            surplus = surplus - extra
    return np.array([most] + counts)


def uneven_parts(rng, count, total, limit, slope):
    if count == 2:
        one = jax.random.randint(rng, (), max(1, total - limit), min(limit, total - 1) + 1)
        return jnp.stack([one, total - one])
    sizes = jnp.asarray(split_up(count, total, limit, slope), jnp.int32)
    pairs = (count - 1) // 2
    donor, sink = sizes[1:1 + 2 * pairs:2], sizes[2:2 + 2 * pairs:2]
    slack = jnp.minimum(donor - 1, limit - sink)
    moved = jax.random.randint(jax.random.fold_in(rng, 1), (pairs,), 0, 1 << 20) % (slack + 1)
    sizes = sizes.at[1:1 + 2 * pairs:2].set(donor - moved).at[2:2 + 2 * pairs:2].set(sink + moved)
    return sizes[jax.random.permutation(jax.random.fold_in(rng, 2), count)]


def assign_block(own_key, own, number, rows, count, top, limit, skew):
    order = jax.random.permutation(own_key, count)
    packed, ordinary = load_shares(count, rows * top, limit, skew, True), load_shares(count, rows * top, limit, skew, False)
    places = jnp.arange(count)

    def named(tallies, rotation):
        used = int((tallies > 0).sum())
        fixed = max(1, used // 4)
        passed = fixed + (places - fixed + rotation * (used - fixed)) % max(1, count - fixed)
        return jnp.zeros((count,), jnp.int32).at[order[jnp.where(places < fixed, places, passed)]].set(jnp.asarray(tallies, jnp.int32))

    tallies = jnp.where(number % 4 == 0, named(packed, number // 4), named(ordinary, number - number // 4 - 1))
    mixed = jax.random.permutation(jax.random.fold_in(own, 3), count)
    source_of, receiver = mixed[0:count // 2 * 2:2], mixed[1:count // 2 * 2:2]
    margin = jnp.minimum(tallies[source_of] - 1, limit - tallies[receiver]) // 2
    margin = jnp.where((source_of == order[0]) | (receiver == order[0]) | (tallies[receiver] == 0), 0, jnp.maximum(margin, 0))
    passed = jax.random.randint(jax.random.fold_in(own, 4), (count // 2,), 0, 1 << 20) % (margin + 1)
    tallies = tallies.at[source_of].add(-passed).at[receiver].add(passed)
    labels = jnp.searchsorted(jnp.cumsum(tallies), jnp.arange(rows * top), side="right").astype(jnp.int32)
    grid = labels.reshape(top, rows).T
    grid = grid[jax.random.permutation(jax.random.fold_in(own, 1), rows)]
    rotation = jax.random.randint(jax.random.fold_in(own, 2), (rows, 1), 0, top)
    return jnp.take_along_axis(grid, (jnp.arange(top)[None, :] + rotation) % top, axis=1)


def load_shares(number_of, total, limit, slope, full):
    loads = [(1 << 20) // math.isqrt(grade ** slope) + 1 for grade in range(1, number_of + 1)]
    largest = limit if full else min(limit, max(-(-total // number_of), total * loads[0] // sum(loads)))
    least = 1 if total - largest >= number_of - 1 else 0
    given, spare = [largest] + [least] * (number_of - 1), total - largest - least * (number_of - 1)
    while spare > 0:
        movable = [i for i in range(1, number_of) if given[i] < largest] or [i for i in range(1, number_of) if given[i] < limit]
        whole, left = sum([loads[i] for i in movable]), spare
        for i in movable:
            addition = min(limit - given[i], max(1, left * loads[i] // whole), spare)
            given[i] = given[i] + addition
            spare = spare - addition
    return np.array(given)


def noise(stream_key, extent, deviation, bound, split=(), held_as=jnp.bfloat16):
    factor_of = shard_levels(stream_key, extent, split, -0.22, 0.18) if split else 1.0
    entries = jax.random.normal(stream_key, extent, jnp.float32) * deviation * factor_of
    return jnp.minimum(jnp.maximum(entries, -bound), bound).astype(held_as)


def setup_inputs(seed: int = 0) -> dict:
    splits = jax.random.split(jax.random.key(seed), 8)
    tokens = noise(splits[0], (TOKENS, D), 1.0, 6.0, ((0, 128), (1, 4)))
    routes_keys = jax.random.split(jax.random.fold_in(splits[1], 1), TOKENS // TOK_DEV)
    routes_turns = jax.random.permutation(jax.random.fold_in(splits[1], 3), TOKENS // TOK_DEV)
    routes = jax.vmap(lambda own, number: assign_block(jax.random.fold_in(splits[1], 2), own, number, TOK_DEV, EXPERTS, TOPW, CAP, 1))(routes_keys, routes_turns).reshape((TOKENS, TOPW))
    gate_prob = jnp.clip(jnp.exp(math.log(1.0) - 2.9957323 * jax.random.uniform(splits[2], (TOKENS, TOPW), jnp.float32) ** shard_levels(splits[2], (TOKENS, TOPW), ((0, 128),), -0.2, 0.2)), 0.05, 1.0)
    token_count = uneven_parts(splits[3], GROUPS, 3 * TOKENS // 4, TOK_DEV, 1).astype(jnp.int32)
    gate_weight = noise(splits[4], (EXPERTS, D, FF), D ** -0.5, 0.09375, ((1, 128), (2, 4)))
    up_weight = noise(splits[5], (EXPERTS, D, FF), D ** -0.5, 0.09375, ((1, 128), (2, 4)))
    down_weight = noise(splits[6], (EXPERTS, D, FF), FF ** -0.5, 0.15625, ((1, 128), (2, 4)))
    return {"tokens": tokens, "routes": routes, "gate_prob": gate_prob, "token_count": token_count, "gate_weight": gate_weight, "up_weight": up_weight, "down_weight": down_weight}


def reference(tokens, routes, gate_prob, token_count, gate_weight, up_weight, down_weight):
    groups = token_count.shape[0]
    tok_dev = tokens.shape[0] // groups
    experts = gate_weight.shape[0]
    top_slots = routes.shape[1]
    model_width = tokens.shape[1]
    hidden_units = gate_weight.shape[2]
    capacity = CAP
    positions = jnp.arange(tok_dev).astype(jnp.int32)
    live_rows = positions[None, :] < token_count[:, None]
    live_pair = jnp.repeat(live_rows, top_slots, axis=1)
    route_flat = routes.reshape(groups, tok_dev * top_slots)
    expert_ids = jnp.arange(experts).astype(jnp.int32)
    one_hot = ((route_flat[:, :, None] == expert_ids[None, None, :]) & live_pair[:, :, None]).astype(jnp.int32)
    pair_rank = jnp.sum((jnp.cumsum(one_hot, axis=1) - one_hot) * one_hot, axis=2).astype(jnp.int32)
    group_ids = jnp.arange(groups).astype(jnp.int32)
    global_tok = (group_ids[:, None] * tok_dev + jnp.repeat(positions, top_slots)[None, :]).astype(jnp.int32)
    slot_expert = jnp.where(live_pair, route_flat, experts).astype(jnp.int32)
    group_index = jnp.broadcast_to(group_ids[:, None], route_flat.shape)
    index_table = jnp.zeros((experts, groups, capacity), jnp.int32)
    weight_table = jnp.zeros((experts, groups, capacity), jnp.float32)
    index_table = index_table.at[slot_expert, group_index, pair_rank].set(global_tok, mode="drop")
    weight_table = weight_table.at[slot_expert, group_index, pair_rank].set(gate_prob.reshape(groups, -1).astype(jnp.float32), mode="drop")
    quarter_width = hidden_units // N_TENSOR

    def one_expert(running, inputs):
        index_rows, weight_rows, w_gate, w_up, w_down = inputs
        flat_index = index_rows.reshape(-1)
        gathered = tokens[flat_index]
        gate_proj = jnp.dot(gathered, w_gate, preferred_element_type=jnp.float32)
        up_proj = jnp.dot(gathered, w_up, preferred_element_type=jnp.float32)
        hidden = (jax.nn.silu(gate_proj) * up_proj).astype(jnp.bfloat16)
        partial_value = jnp.zeros((gathered.shape[0], model_width), jnp.float32)
        for quarter_index in range(N_TENSOR):
            low = quarter_index * quarter_width
            term_piece = lax.dot_general(hidden[:, low:low + quarter_width], w_down[:, low:low + quarter_width], (((1,), (1,)), ((), ())), preferred_element_type=jnp.float32)
            rounded = lax.optimization_barrier(term_piece.astype(jnp.bfloat16))
            partial_value = partial_value + rounded.astype(jnp.float32)
        result = lax.optimization_barrier(partial_value.astype(jnp.bfloat16)).astype(jnp.float32)
        running = running.at[flat_index].add(weight_rows.reshape(-1)[:, None] * result)
        return running, jnp.zeros((), jnp.float32)

    start_total = jnp.zeros((tokens.shape[0], model_width), jnp.float32)
    running, unused = lax.scan(one_expert, start_total, (index_table, weight_table, gate_weight, up_weight, down_weight))
    return running.astype(jnp.bfloat16)
```

```python
import functools

import jax
import jax.numpy as jnp
from jax import lax
from jax.experimental import pallas as pl
from jax.experimental.pallas import tpu as pltpu
from jax.sharding import PartitionSpec as P

MESH = pl.DeviceIdType.MESH
BF16 = jnp.bfloat16
F32 = jnp.float32


class Place:
    def __init__(self, nx, ny, nz, nzl):
        self.nx, self.ny, self.nz, self.nzl = nx, ny, nz, nzl
        self.nzh = nz // nzl

    def here(self):
        e = lax.axis_index("expert")
        x = lax.axis_index("tensor")
        zl = lax.axis_index("dp")
        core = lax.rem(e, 2)
        zh = lax.rem(e // 2, self.nzh)
        y = e // (2 * self.nzh)
        return x, y, zh * self.nzl + zl, core

    def dev(self, x, y, z, core):
        zh = z // self.nzl
        zl = lax.rem(z, self.nzl)
        return ((y * self.nzh + zh) * 2 + core, x, zl)


def signal_all(pos, x, y, z, c, barrier, xy, zring, core):
    n = 0
    if core:
        pl.semaphore_signal(barrier, inc=1, device_id=pos.dev(x, y, z, 1 - c), device_id_type=MESH)
        n += 1
    if zring == "ring":
        for dz in (1, pos.nz - 1):
            zz = lax.rem(z + dz, pos.nz)
            pl.semaphore_signal(barrier, inc=1, device_id=pos.dev(x, y, zz, c), device_id_type=MESH)
        n += 2
    if zring == "all":

        def zbody(k, carry):
            zz = lax.rem(z + k, pos.nz)
            pl.semaphore_signal(barrier, inc=1, device_id=pos.dev(x, y, zz, c), device_id_type=MESH)
            return carry

        lax.fori_loop(1, pos.nz, zbody, 0)
        n += pos.nz - 1
    if xy:

        def body(k, carry):
            xx = lax.rem(x + lax.rem(k, pos.nx), pos.nx)
            yy = lax.rem(y + k // pos.nx, pos.ny)
            pl.semaphore_signal(barrier, inc=1, device_id=pos.dev(xx, yy, z, c), device_id_type=MESH)
            return carry

        lax.fori_loop(1, pos.nx * pos.ny, body, 0)
        n += pos.nx * pos.ny - 1
    pl.semaphore_wait(barrier, n)


def z_exchange_kernel(pos, n, refs):
    srcs, dsts = refs[:n], refs[n : 2 * n]
    send, recv, loc = refs[2 * n : 2 * n + 3]
    x, y, z, c = pos.here()
    signal_all(pos, x, y, z, c, pltpu.get_barrier_semaphore(), False, "all", False)

    def body(k, carry):
        zz = lax.rem(z + k, pos.nz)
        for i in range(n):
            pltpu.make_async_remote_copy(
                srcs[i].at[zz], dsts[i].at[z], send.at[i], recv.at[i], device_id=pos.dev(x, y, zz, c), device_id_type=MESH
            ).start()
        return carry

    lax.fori_loop(1, pos.nz, body, 0)
    for i in range(n):
        pltpu.make_async_copy(srcs[i].at[z], dsts[i].at[z], loc.at[i]).start()
    for i in range(n):
        pltpu.make_async_copy(srcs[i].at[z], dsts[i].at[z], loc.at[i]).wait()
        part = dsts[i].at[pl.ds(0, pos.nz - 1)]
        pltpu.make_async_copy(part, part, send.at[i]).wait()
        pltpu.make_async_copy(part, part, recv.at[i]).wait()


def z_exchange(pos, cid, *arrays):
    n = len(arrays)
    any_spec = pl.BlockSpec(memory_space=pl.ANY)
    return pl.pallas_call(
        lambda *refs: z_exchange_kernel(pos, n, refs),
        out_shape=[jax.ShapeDtypeStruct(a.shape, a.dtype) for a in arrays],
        in_specs=[any_spec] * n,
        out_specs=[any_spec] * n,
        scratch_shapes=[pltpu.SemaphoreType.DMA((n,)), pltpu.SemaphoreType.DMA((n,)), pltpu.SemaphoreType.DMA((n,))],
        compiler_params=pltpu.CompilerParams(collective_id=cid, has_side_effects=True),
        name="z_exchange",
    )(*arrays)


class WeightRelay:
    def __init__(self, pos, src, dst, send, recv, fsend, frecv, loc):
        self.pos, self.src, self.dst = pos, src, dst
        self.send, self.recv, self.fsend, self.frecv, self.loc = send, recv, fsend, frecv, loc
        self.width = src.shape[2]

    def slot(self, x, y, c):
        cols = pl.ds(pl.multiple_of(x * self.width, self.width), self.width)
        return self.dst.at[y, c, :, cols]

    def start_one(self, k, me):
        pos = self.pos
        x, y, z, c = me
        xx = lax.rem(x + lax.rem(k, pos.nx), pos.nx)
        yy = lax.rem(y + k // pos.nx, pos.ny)
        pltpu.make_async_remote_copy(
            self.src.at[yy * pos.nx + xx],
            self.slot(x, y, c),
            self.send,
            self.recv.at[k],
            device_id=pos.dev(xx, yy, z, c),
            device_id_type=MESH,
        ).start()

    def start_own(self, me):
        pos = self.pos
        x, y, z, c = me
        own = self.src.at[y * pos.nx + x]
        pltpu.make_async_copy(own, self.slot(x, y, c), self.loc).start()
        pltpu.make_async_remote_copy(
            own, self.slot(x, y, c), self.fsend, self.frecv, device_id=pos.dev(x, y, z, 1 - c), device_id_type=MESH
        ).start()

    def forward_one(self, k, me):
        pos = self.pos
        x, y, z, c = me
        xs = lax.rem(x - lax.rem(k, pos.nx) + pos.nx, pos.nx)
        ys = lax.rem(y - k // pos.nx + pos.ny, pos.ny)
        block = self.slot(xs, ys, c)
        pltpu.make_async_copy(block, block, self.recv.at[k]).wait()
        pltpu.make_async_remote_copy(
            block, block, self.fsend, self.frecv, device_id=pos.dev(x, y, z, 1 - c), device_id_type=MESH
        ).start()

    def finish(self, me):
        x, y, z, c = me
        own = self.src.at[y * self.pos.nx + x]
        pltpu.make_async_copy(own, self.slot(x, y, c), self.loc).wait()
        sent = self.src.at[pl.ds(0, self.pos.nx * self.pos.ny - 1)]
        pltpu.make_async_copy(sent, sent, self.send).wait()
        whole = self.dst.at[:, 0]
        pltpu.make_async_copy(whole, whole, self.fsend).wait()
        pltpu.make_async_copy(whole, whole, self.frecv).wait()


class SlotExchange:
    def __init__(self, pos, src_at, dst_at, all_but_one, send, recv, loc):
        self.pos, self.src_at, self.dst_at, self.part = pos, src_at, dst_at, all_but_one
        self.send, self.recv, self.loc = send, recv, loc

    def start_one(self, k, me):
        pos = self.pos
        x, y, z, c = me
        xx = lax.rem(x + lax.rem(k, pos.nx), pos.nx)
        yy = lax.rem(y + k // pos.nx, pos.ny)
        pltpu.make_async_remote_copy(
            self.src_at(xx, yy), self.dst_at(x, y), self.send, self.recv, device_id=pos.dev(xx, yy, z, c), device_id_type=MESH
        ).start()

    def start_own(self, me):
        x, y, z, c = me
        pltpu.make_async_copy(self.src_at(x, y), self.dst_at(x, y), self.loc).start()

    def finish(self, me):
        x, y, z, c = me
        pltpu.make_async_copy(self.src_at(x, y), self.dst_at(x, y), self.loc).wait()
        pltpu.make_async_copy(self.part, self.part, self.send).wait()
        pltpu.make_async_copy(self.part, self.part, self.recv).wait()


def tokens_and_weights(pos, cid, slots, w_gate, w_up):
    nxy = pos.nx * pos.ny
    _, rows, feat = slots.shape
    _, depth, width = w_gate.shape

    def kernel(slots_ref, wg_ref, wu_ref, x_ref, g_ref, u_ref, sends, recvs, locs, wrecv, fsend, frecv):
        me = pos.here()
        x, y, z, c = me
        signal_all(pos, x, y, z, c, pltpu.get_barrier_semaphore(), True, None, True)
        ex = SlotExchange(
            pos,
            lambda xx, yy: slots_ref.at[yy * pos.nx + xx],
            lambda xx, yy: x_ref.at[yy, :, pl.ds(pl.multiple_of(xx * feat, feat), feat)],
            slots_ref.at[pl.ds(0, nxy - 1)],
            sends.at[0],
            recvs.at[0],
            locs.at[0],
        )
        relays = [
            WeightRelay(pos, wg_ref, g_ref, sends.at[1], wrecv.at[0], fsend.at[0], frecv.at[0], locs.at[1]),
            WeightRelay(pos, wu_ref, u_ref, sends.at[2], wrecv.at[1], fsend.at[1], frecv.at[1], locs.at[2]),
        ]

        def start(k, carry):
            for r in relays:
                r.start_one(k, me)
            ex.start_one(k, me)
            return carry

        lax.fori_loop(1, nxy, start, 0)
        ex.start_own(me)
        for r in relays:
            r.start_own(me)

        def forward(k, carry):
            for r in relays:
                r.forward_one(k, me)
            return carry

        lax.fori_loop(1, nxy, forward, 0)
        ex.finish(me)
        for r in relays:
            r.finish(me)

    any_spec = pl.BlockSpec(memory_space=pl.ANY)
    w_shape = jax.ShapeDtypeStruct((pos.ny, 2, depth, pos.nx * width), BF16)
    return pl.pallas_call(
        kernel,
        out_shape=[jax.ShapeDtypeStruct((pos.ny, rows, pos.nx * feat), BF16), w_shape, w_shape],
        in_specs=[any_spec] * 3,
        out_specs=[any_spec] * 3,
        scratch_shapes=[
            pltpu.SemaphoreType.DMA((3,)),
            pltpu.SemaphoreType.DMA((1,)),
            pltpu.SemaphoreType.DMA((3,)),
            pltpu.SemaphoreType.DMA((2, nxy)),
            pltpu.SemaphoreType.DMA((2,)),
            pltpu.SemaphoreType.DMA((2,)),
        ],
        compiler_params=pltpu.CompilerParams(collective_id=cid, has_side_effects=True),
        name="tokens_and_weights",
    )(slots, w_gate, w_up)


def reduce_and_gather(pos, cid, part_gate, part_up, w_down):
    nz = pos.nz
    nxy = pos.nx * pos.ny
    _, rows, cols = part_gate.shape
    _, depth, width = w_down.shape
    subs = 2
    half = cols // subs

    def kernel(g_ref, u_ref, wd_ref, h_ref, d_ref, land, rs_send, rs_recv, ag_send, ag_recv, sems, wrecv):
        me = pos.here()
        x, y, z, c = me
        signal_all(pos, x, y, z, c, pltpu.get_barrier_semaphore(), True, "ring", True)
        relay = WeightRelay(pos, wd_ref, d_ref, sems.at[0], wrecv, sems.at[1], sems.at[2], sems.at[3])
        after, before = lax.rem(z + 1, nz), lax.rem(z + nz - 1, nz)
        target = (pos.dev(x, y, after, c), pos.dev(x, y, before, c))
        parts = (g_ref, u_ref)

        def chunk(d, s):
            return lax.rem(z - s - 1 + 2 * nz, nz) if d == 0 else lax.rem(z + s + 1, nz)

        def rs_copy(d, sub, s, src):
            return pltpu.make_async_remote_copy(
                src, land.at[d, s, sub], rs_send.at[d, sub, s], rs_recv.at[d, sub, s], device_id=target[d], device_id_type=MESH
            )

        def cut(ref, j, sub):
            return ref.at[j, :, pl.ds(sub * half, half)]

        for sub in range(subs):
            for d in range(2):
                rs_copy(d, sub, 0, cut(parts[d], chunk(d, 0), sub)).start()

        def start(k, carry):
            relay.start_one(k, me)
            return carry

        lax.fori_loop(1, nxy, start, 0)
        relay.start_own(me)

        def rs_step(s, carry):
            for sub in range(subs):
                for d in range(2):
                    slot = land.at[d, s, sub]
                    pltpu.make_async_copy(slot, slot, rs_recv.at[d, sub, s]).wait()
                    mine = parts[d][chunk(d, s + 1), :, pl.ds(sub * half, half)]
                    slot[...] = (slot[...].astype(F32) + mine.astype(F32)).astype(BF16)
                    rs_copy(d, sub, s + 1, slot).start()
            return carry

        lax.fori_loop(0, nz - 2, rs_step, 0)

        def ag_copy(d, j, s):
            block = h_ref.at[j, :, pl.ds(d * half, half)]
            return pltpu.make_async_remote_copy(
                block, block, ag_send.at[d, s], ag_recv.at[d, s], device_id=target[d], device_id_type=MESH
            )

        last = nz - 2
        for sub in range(subs):
            total = []
            for d in range(2):
                slot = land.at[d, last, sub]
                pltpu.make_async_copy(slot, slot, rs_recv.at[d, sub, last]).wait()
                mine = parts[d][z, :, pl.ds(sub * half, half)]
                total.append(slot[...].astype(F32) + mine.astype(F32))
            gate, up = total
            h_ref[z, :, pl.ds(sub * half, half)] = (gate / (1.0 + jnp.exp(-gate)) * up).astype(BF16)
            ag_copy(sub, z, 0).start()

        def ag_index(d, s):
            return lax.rem(z - s + nz, nz) if d == 0 else lax.rem(z + s, nz)

        def ag_step(s, carry):
            for d in range(2):
                j = ag_index(d, s + 1)
                block = h_ref.at[j, :, pl.ds(d * half, half)]
                pltpu.make_async_copy(block, block, ag_recv.at[d, s]).wait()

                ag_copy(d, j, s + 1).start()
            return carry

        lax.fori_loop(0, nz - 2, ag_step, 0)

        def forward(k, carry):
            relay.forward_one(k, me)
            return carry

        lax.fori_loop(1, nxy, forward, 0)
        relay.finish(me)
        for d in range(2):
            block = h_ref.at[0, :, pl.ds(d * half, half)]
            pltpu.make_async_copy(block, block, ag_recv.at[d, nz - 2]).wait()

        def drain(s, carry):
            for d in range(2):
                for sub in range(subs):
                    slot = land.at[d, s, sub]
                    pltpu.make_async_copy(slot, slot, rs_send.at[d, sub, s]).wait()
                block = h_ref.at[0, :, pl.ds(d * half, half)]
                pltpu.make_async_copy(block, block, ag_send.at[d, s]).wait()
            return carry

        lax.fori_loop(0, nz - 1, drain, 0)

    any_spec = pl.BlockSpec(memory_space=pl.ANY)
    vmem = pl.BlockSpec(memory_space=pltpu.VMEM)
    return pl.pallas_call(
        kernel,
        out_shape=[
            jax.ShapeDtypeStruct((nz, rows, cols), BF16),
            jax.ShapeDtypeStruct((pos.ny, 2, depth, pos.nx * width), BF16),
        ],
        in_specs=[vmem, vmem, any_spec],
        out_specs=[vmem, any_spec],
        scratch_shapes=[
            pltpu.VMEM((2, nz - 1, subs, rows, half), BF16),
            pltpu.SemaphoreType.DMA((2, subs, nz - 1)),
            pltpu.SemaphoreType.DMA((2, subs, nz - 1)),
            pltpu.SemaphoreType.DMA((2, nz - 1)),
            pltpu.SemaphoreType.DMA((2, nz - 1)),
            pltpu.SemaphoreType.DMA((4,)),
            pltpu.SemaphoreType.DMA((nxy,)),
        ],
        compiler_params=pltpu.CompilerParams(collective_id=cid, has_side_effects=True),
        name="reduce_and_gather",
    )(part_gate, part_up, w_down)


def slots_back(pos, cid, out):
    nxy = pos.nx * pos.ny
    _, rows, cols = out.shape
    feat = cols // pos.nx

    def kernel(o_ref, r_ref, sems):
        me = pos.here()
        x, y, z, c = me
        signal_all(pos, x, y, z, c, pltpu.get_barrier_semaphore(), True, None, False)
        ex = SlotExchange(
            pos,
            lambda xx, yy: o_ref.at[yy, :, pl.ds(pl.multiple_of(xx * feat, feat), feat)],
            lambda xx, yy: r_ref.at[yy * pos.nx + xx],
            r_ref.at[pl.ds(0, nxy - 1)],
            sems.at[0],
            sems.at[1],
            sems.at[2],
        )

        def start(k, carry):
            ex.start_one(k, me)
            return carry

        lax.fori_loop(1, nxy, start, 0)
        ex.start_own(me)
        ex.finish(me)

    any_spec = pl.BlockSpec(memory_space=pl.ANY)
    return pl.pallas_call(
        kernel,
        out_shape=jax.ShapeDtypeStruct((nxy, rows, feat), BF16),
        in_specs=[any_spec],
        out_specs=any_spec,
        scratch_shapes=[pltpu.SemaphoreType.DMA((3,))],
        compiler_params=pltpu.CompilerParams(collective_id=cid, has_side_effects=True),
        name="slots_back",
    )(out)


def shards(pos, tokens, routes, gate_prob, token_count, gate_weight, up_weight, down_weight):
    experts, depth, width = gate_weight.shape
    nx, nz, nzl = pos.nx, pos.nz, pos.nzl
    nzh = nz // nzl
    tok, feats = tokens.shape
    top = routes.shape[1]
    cap = min(tok, tok * top * 5 // (4 * experts))
    piece = feats // nz
    group_y = feats // (depth * 2 * nz)

    new = jnp.arange(feats, dtype=jnp.int32)
    zz, rest = new // piece, new % piece
    ylo, core, row = rest // (2 * depth), rest // depth % 2, rest % depth
    old = (((ylo * nzh + zz // nzl) * 2 + core) * nzl + zz % nzl) * depth + row
    shuffle = (jnp.arange(feats, dtype=jnp.int32)[:, None] == old[None, :]).astype(BF16)
    by_z = jnp.dot(tokens, shuffle, preferred_element_type=F32).astype(BF16)
    by_z = jnp.stack([by_z[:, i * piece : (i + 1) * piece] for i in range(nz)])

    x, y, z, c = pos.here()
    positions = jnp.arange(tok, dtype=jnp.int32)
    live = positions < token_count[0]
    names = routes.T
    expert_ids = jnp.arange(experts, dtype=jnp.int32)
    named = [(expert_ids[:, None] == names[s][None, :]) & live[None, :] for s in range(top)]
    either = functools.reduce(jnp.logical_or, named).astype(BF16)
    earlier = (positions[:, None] < positions[None, :]).astype(BF16)
    rank = jnp.dot(either, earlier, preferred_element_type=F32).astype(jnp.int32)
    lines = []
    for s in range(top):
        place = (expert_ids[:, None] * nz + z) * cap + rank
        lines.append(jnp.sum(jnp.where(named[s], place + 1, 0), axis=0).astype(F32) - 1.0)
    lines += [gate_prob[:, s] for s in range(top)]
    meta = jnp.concatenate([jnp.stack(lines), jnp.zeros((8 - 2 * top, tok), F32)])
    meta = jnp.broadcast_to(meta[None], (nz, 8, tok))

    raw, infos = z_exchange(pos, 1, by_z, meta)

    slots_all = experts * nz * cap
    slot_of = [infos[:, s].astype(jnp.int32).reshape(nz * tok) for s in range(top)]
    slot_ids = jnp.arange(slots_all, dtype=jnp.int32)
    pick = functools.reduce(jnp.logical_or, [slot_ids[:, None] == s[None, :] for s in slot_of]).astype(BF16)
    outgoing = jnp.dot(pick, raw.reshape(nz * tok, piece), preferred_element_type=F32).astype(BF16)

    rows_in, w_gate, w_up = tokens_and_weights(pos, 2, outgoing.reshape(experts, nz * cap, piece), gate_weight, up_weight)

    depth_all = pos.ny * 2 * depth
    ff = nx * width
    flat = rows_in.reshape(pos.ny * nz * cap, nx * piece)
    gate = jnp.dot(flat, w_gate.reshape(depth_all, ff), preferred_element_type=F32).astype(BF16)
    up = jnp.dot(flat, w_up.reshape(depth_all, ff), preferred_element_type=F32).astype(BF16)
    chunk = flat.shape[0] // nz
    hidden, w_down = reduce_and_gather(
        pos, 3, gate.reshape(nz, chunk, ff), up.reshape(nz, chunk, ff), down_weight
    )
    out = lax.dot_general(
        hidden.reshape(nz * chunk, ff),
        w_down.reshape(depth_all, ff),
        (((1,), (1,)), ((), ())),
        preferred_element_type=F32,
    ).astype(BF16)
    back = slots_back(pos, 4, out.reshape(pos.ny, nz * cap, depth_all))
    back = back.reshape(slots_all, piece)
    mixed = jnp.zeros((nz * tok, piece), F32)
    for s in range(top):
        chosen = (slot_of[s][:, None] == slot_ids[None, :]).astype(BF16)
        prob = infos[:, top + s].reshape(nz * tok)
        mixed = mixed + prob[:, None] * jnp.dot(chosen, back, preferred_element_type=F32)
    (home,) = z_exchange(pos, 5, mixed.astype(BF16).reshape(nz, tok, piece))
    merged = jnp.concatenate([home[i] for i in range(nz)], axis=1)
    unshuffle = (old[:, None] == jnp.arange(feats, dtype=jnp.int32)[None, :]).astype(BF16)
    return jnp.dot(merged, unshuffle, preferred_element_type=F32).astype(BF16)


def solution(mesh):
    nzl = mesh.shape["dp"]
    nx = mesh.shape["tensor"]
    nzh = 2
    ny = mesh.shape["expert"] // (2 * nzh)
    pos = Place(nx, ny, nzh * nzl, nzl)
    in_specs = (
        P(("expert", "dp"), "tensor"),
        P(("expert", "dp"), None),
        P(("expert", "dp"), None),
        P(("expert", "dp")),
        P(None, ("expert", "dp"), "tensor"),
        P(None, ("expert", "dp"), "tensor"),
        P(None, ("expert", "dp"), "tensor"),
    )
    out_specs = P(("expert", "dp"), "tensor")
    return jax.shard_map(
        functools.partial(shards, pos), mesh=mesh, in_specs=in_specs, out_specs=out_specs, check_vma=False
    )
```

```python
import functools

import jax
import jax.numpy as jnp
from jax import lax
from jax.experimental import pallas as pl
from jax.experimental.pallas import tpu as pltpu
from jax.sharding import PartitionSpec as P

MESH = pl.DeviceIdType.MESH
BF16 = jnp.bfloat16
F32 = jnp.float32


class Place:
    def __init__(self, nx, ny, nz, nzl):
        self.nx, self.ny, self.nz, self.nzl = nx, ny, nz, nzl
        self.nzh = nz // nzl

    def here(self):
        e = lax.axis_index("expert")
        x = lax.axis_index("tensor")
        zl = lax.axis_index("dp")
        core = lax.rem(e, 2)
        zh = lax.rem(e // 2, self.nzh)
        y = e // (2 * self.nzh)
        return x, y, zh * self.nzl + zl, core

    def dev(self, x, y, z, core):
        zh = z // self.nzl
        zl = lax.rem(z, self.nzl)
        return ((y * self.nzh + zh) * 2 + core, x, zl)


def signal_all(pos, x, y, z, c, barrier, xy, zring, core):
    n = 0
    if core:
        pl.semaphore_signal(barrier, inc=1, device_id=pos.dev(x, y, z, 1 - c), device_id_type=MESH)
        n += 1
    if zring == "ring":
        for dz in (1, pos.nz - 1):
            zz = lax.rem(z + dz, pos.nz)
            pl.semaphore_signal(barrier, inc=1, device_id=pos.dev(x, y, zz, c), device_id_type=MESH)
        n += 2
    if zring == "all":

        def zbody(k, carry):
            zz = lax.rem(z + k, pos.nz)
            pl.semaphore_signal(barrier, inc=1, device_id=pos.dev(x, y, zz, c), device_id_type=MESH)
            return carry

        lax.fori_loop(1, pos.nz, zbody, 0)
        n += pos.nz - 1
    if xy:

        def body(k, carry):
            xx = lax.rem(x + lax.rem(k, pos.nx), pos.nx)
            yy = lax.rem(y + k // pos.nx, pos.ny)
            pl.semaphore_signal(barrier, inc=1, device_id=pos.dev(xx, yy, z, c), device_id_type=MESH)
            return carry

        lax.fori_loop(1, pos.nx * pos.ny, body, 0)
        n += pos.nx * pos.ny - 1
    pl.semaphore_wait(barrier, n)


def relay_kernel(pos, dims, refs):
    nx, ny, nz = pos.nx, pos.ny, pos.nz
    nxy = nx * ny
    parts, cap8, piece, top = dims["parts"], dims["rows"], dims["piece"], dims["top"]
    depth, lane = dims["depth"], dims["lane"]
    rows = cap8
    half = nx * lane // 2
    (tok_ref, meta_ref, wg_ref, wu_ref, wd_ref, back_ref, info_ref) = refs[:7]
    (raw, out_tok, x_in, wbuf, part, land, hid, acc, out) = refs[7:16]
    (zsend, zrecv, loc, wsend, wrecv, fsend, frecv, tsend, trecv, rsend, rrecv, asend, arecv, bsem) = refs[16:]
    me = pos.here()
    x, y, z, c = me
    weights = (wg_ref, wu_ref, wd_ref)
    partner = pos.dev(x, y, z, 1 - c)

    def remote(src, dst, s, r, dev):
        return pltpu.make_async_remote_copy(src, dst, s, r, device_id=dev, device_id_type=MESH)

    def wait(ref, sem):
        pltpu.make_async_copy(ref, ref, sem).wait()

    signal_all(pos, x, y, z, c, pltpu.get_barrier_semaphore(), True, "all", True)

    def raw_send(k, carry):
        zz = lax.rem(z + k, nz)
        dev = pos.dev(x, y, zz, c)
        cols = pl.ds(pl.multiple_of(zz * piece, piece), piece)
        remote(meta_ref, info_ref.at[z], zsend.at[1], zrecv.at[1], dev).start()
        remote(tok_ref.at[:, cols], raw.at[z], zsend.at[0], zrecv.at[0], dev).start()
        return carry

    lax.fori_loop(1, nz, raw_send, 0)
    own_cols = pl.ds(pl.multiple_of(z * piece, piece), piece)
    own_raw = pltpu.make_async_copy(tok_ref.at[:, own_cols], raw.at[z], loc.at[0])
    own_meta = pltpu.make_async_copy(meta_ref, info_ref.at[z], loc.at[1])
    own_raw.start()
    own_meta.start()

    def w_src(m, w, e):
        return weights[m].at[e, :, pl.ds(w * lane, lane)]

    def w_dst(m, w, xs, ys, cs):
        return wbuf.at[w, m, ys, cs, :, pl.ds(pl.multiple_of(xs * lane, lane), lane)]

    def w_start(w, mats):
        def body(k, carry):
            xx = lax.rem(x + lax.rem(k, nx), nx)
            yy = lax.rem(y + k // nx, ny)
            dev = pos.dev(xx, yy, z, c)
            for m in mats:
                remote(w_src(m, w, yy * nx + xx), w_dst(m, w, x, y, c), wsend.at[m, w], wrecv.at[m, w], dev).start()
            return carry

        lax.fori_loop(1, nxy, body, 0)
        for m in mats:
            pltpu.make_async_copy(w_src(m, w, y * nx + x), w_dst(m, w, x, y, c), loc.at[2 + 3 * w + m]).start()

    def w_forward(w, mats):
        for m in mats:
            pltpu.make_async_copy(w_src(m, w, y * nx + x), w_dst(m, w, x, y, c), loc.at[2 + 3 * w + m]).wait()
            wait(weights[m].at[pl.ds(0, nxy - 1), :, pl.ds(w * lane, lane)], wrecv.at[m, w])
            block = wbuf.at[w, m, :, c]
            remote(block, block, fsend.at[m, w], frecv.at[m, w], partner).start()

    def w_ready(w, mats):
        for m in mats:
            wait(wbuf.at[w, m, :, 0], frecv.at[m, w])

    w_start(0, (0, 1))

    own_raw.wait()
    own_meta.wait()
    for i, ref in ((1, info_ref), (0, raw)):
        wait(ref.at[pl.ds(0, nz - 1)], zsend.at[i])
        wait(ref.at[pl.ds(0, nz - 1)], zrecv.at[i])
    count = nx * rows

    def dispatch(dy):
        yy = lax.rem(y + dy, ny)
        ids = lax.broadcasted_iota(jnp.int32, (count, raw.shape[1]), 0).astype(F32)
        base = (yy * count).astype(F32)
        picks = []
        for zz in range(nz):
            hit = None
            for s in range(top):
                same = ids == (info_ref[zz, s : s + 1, :] - base)
                hit = same if hit is None else hit | same
            picks.append(jnp.where(hit, 1.0, 0.0).astype(BF16))
        pick = jnp.concatenate(picks, axis=1)
        feats = raw[...].reshape(nz * raw.shape[1], piece)
        got = jnp.dot(pick, feats, preferred_element_type=F32).astype(BF16)
        out_tok[pl.ds(yy * nx, nx)] = got.reshape(nx, rows, piece)

    def t_dst(xs, ys):
        return x_in.at[ys, :, pl.ds(pl.multiple_of(xs * piece, piece), piece)]

    def t_send(dy, first):
        yy = lax.rem(y + dy, ny)
        for dx in range(first, nx):
            xx = lax.rem(x + dx, nx)
            remote(out_tok.at[yy * nx + xx], t_dst(x, y), tsend, trecv, pos.dev(xx, yy, z, c)).start()

    dispatch(1)

    def d_body(dy, carry):
        dispatch(dy)
        t_send(dy - 1, 0)
        return carry

    lax.fori_loop(2, ny, d_body, 0)
    dispatch(0)
    t_send(ny - 1, 0)
    w_start(1, (0, 1))
    t_send(0, 1)
    own_tok = pltpu.make_async_copy(out_tok.at[y * nx + x], t_dst(x, y), loc.at[11])
    own_tok.start()
    w_forward(0, (0, 1))

    def product(w):
        wide = nx * lane
        for m in range(2):
            right = wbuf[w, m].reshape(ny * 2 * depth, wide)

            def body(i, carry):
                left = x_in[pl.ds(i * (ny // 2), ny // 2)].reshape(ny // 2 * rows, nx * piece)
                res = jnp.dot(left, right, preferred_element_type=F32).astype(BF16)
                part[w, pl.ds(i * (ny // 2), ny // 2), :, m * wide : (m + 1) * wide] = res.reshape(ny // 2, rows, wide)
                return carry

            lax.fori_loop(0, 2, body, 0)

    step = (1, nz - 1)
    near = (pos.dev(x, y, lax.rem(z + 1, nz), c), pos.dev(x, y, lax.rem(z + nz - 1, nz), c))
    far = nz // 2
    chains = [(d, h, far if h == d else far - 1) for h in range(2) for d in range(2)]
    wide = nx * lane

    def at(d, k):
        return lax.rem(z + (k if d == 0 else -k) + 2 * nz, nz)

    def rs_send(w, d, h, i, src):
        remote(src, land.at[w, d, h, i], rsend.at[w, d, h, i], rrecv.at[w, d, h, i], near[d]).start()

    def rs_start(w):
        for d, h, n in chains:
            rs_send(w, d, h, 0, part.at[w, at(d, n), :, pl.ds(h * wide, wide)])

    def rs_mid(w, i):
        for d, h, n in chains:
            if i < n:
                slot = land.at[w, d, h, i - 1]
                wait(slot, rrecv.at[w, d, h, i - 1])
                mine = part[w, at(d, n - i), :, pl.ds(h * wide, wide)]
                slot[...] = (slot[...].astype(F32) + mine.astype(F32)).astype(BF16)
        for d, h, n in chains:
            if i < n:
                rs_send(w, d, h, i, land.at[w, d, h, i - 1])

    def ag_send(w, d, h, i, j):
        block = hid.at[w, j, :, pl.ds(h * half, half)]
        remote(block, block, asend.at[w, d, h, i], arecv.at[w, d, h, i], near[d]).start()

    def rs_final(w):
        total = []
        for h in range(2):
            t = part[w, z, :, pl.ds(h * wide, wide)].astype(F32)
            for d, hh, n in chains:
                if hh == h:
                    slot = land.at[w, d, h, n - 1]
                    wait(slot, rrecv.at[w, d, h, n - 1])
                    t = t + slot[...].astype(F32)
            total.append(t)
        gate, up = total
        hid[w, z] = (gate / (1.0 + jnp.exp(-gate)) * up).astype(BF16)

    def ag_start(w):
        for d, h, n in chains:
            ag_send(w, d, h, 0, z)

    def ag_mid(w, i):
        for d, h, n in chains:
            if i <= n:
                j = at(d, -i)
                wait(hid.at[w, j, :, pl.ds(h * half, half)], arecv.at[w, d, h, i - 1])
                if i < n:
                    ag_send(w, d, h, i, j)

    def down(w, left):
        return lax.dot_general(
            left, wbuf[w, 2].reshape(ny * 2 * depth, wide), (((1,), (1,)), ((), ())), preferred_element_type=F32
        )

    def accumulate(w):
        def body(i, carry):
            span = pl.ds(i * (nz // 2), nz // 2)
            res = down(w, hid[w, span].reshape(nz // 2 * rows, wide)).reshape(nz // 2, rows, ny * 2 * depth)
            acc[span] = res if w == 0 else acc[span] + res
            return carry

        lax.fori_loop(0, 2, body, 0)

    def o_src(xx, j):
        return out.at[j, :, pl.ds(pl.multiple_of(xx * piece, piece), piece)]

    def finish_rows(js):
        last = parts - 1
        left = jnp.concatenate([hid[last, j] for j in js], axis=0) if len(js) > 1 else hid[last, js[0]]
        res = down(last, left)
        for i, j in enumerate(js):
            out[j] = (acc[j] + res[i * rows : (i + 1) * rows]).astype(BF16)

    def send_rows(js):
        for j in js:
            for dx in range(nx):
                xx = lax.rem(x + dx, nx)
                away = remote(o_src(xx, j), back_ref.at[y * nx + x], bsem.at[0], bsem.at[1], pos.dev(xx, j, z, c))
                if dx:
                    away.start()
                else:

                    @pl.when(j != y)
                    def _():
                        away.start()

                    @pl.when(j == y)
                    def _():
                        pltpu.make_async_copy(o_src(x, y), back_ref.at[y * nx + x], bsem.at[2]).start()

    own_tok.wait()
    wait(out_tok.at[pl.ds(0, nxy - 1)], tsend)
    wait(out_tok.at[pl.ds(0, nxy - 1)], trecv)
    w_ready(0, (0, 1))
    product(0)
    rs_start(0)
    w_start(2, (0, 1))
    rs_mid(0, 1)
    w_forward(1, (0, 1))
    rs_mid(0, 2)
    w_ready(1, (0, 1))
    product(1)
    rs_start(1)
    for w in range(parts):
        w_start(w, (2,))
    rs_mid(0, 3)
    rs_mid(1, 1)
    rs_final(0)
    w_forward(2, (0, 1))
    ag_start(0)
    rs_mid(1, 2)
    w_ready(2, (0, 1))
    product(2)
    rs_start(2)
    ag_mid(0, 1)
    rs_mid(1, 3)
    rs_mid(2, 1)
    ag_mid(0, 2)
    rs_final(1)
    ag_start(1)
    rs_mid(2, 2)
    ag_mid(0, 3)
    ag_mid(1, 1)
    w_forward(0, (2,))
    rs_mid(2, 3)
    ag_mid(0, 4)
    ag_mid(1, 2)
    w_ready(0, (2,))
    accumulate(0)
    rs_final(2)
    w_forward(1, (2,))
    ag_start(2)
    ag_mid(1, 3)
    w_forward(2, (2,))
    ag_mid(1, 4)
    w_ready(1, (2,))
    w_ready(2, (2,))
    ag_mid(2, 1)
    accumulate(1)
    finish_rows([z])
    ag_mid(2, 2)
    finish_rows([at(0, 1), at(1, 1)])
    send_rows([z])
    ag_mid(2, 3)
    finish_rows([at(0, 2), at(1, 2)])
    send_rows([at(0, 1), at(1, 1)])
    ag_mid(2, 4)
    finish_rows([at(0, 3), at(1, 3)])
    send_rows([at(0, 2), at(1, 2)])
    finish_rows([at(0, 4)])
    send_rows([at(0, 3), at(1, 3), at(0, 4)])

    for m in range(3):
        for w in range(parts):
            wait(weights[m].at[pl.ds(0, nxy - 1), :, pl.ds(w * lane, lane)], wsend.at[m, w])
            wait(wbuf.at[w, m, :, 0], fsend.at[m, w])
    for w in range(parts):
        for d, h, n in chains:
            for i in range(n):
                wait(land.at[w, d, h, i], rsend.at[w, d, h, i])
                wait(hid.at[w, z, :, pl.ds(h * half, half)], asend.at[w, d, h, i])
    pltpu.make_async_copy(o_src(x, y), back_ref.at[y * nx + x], bsem.at[2]).wait()
    wait(back_ref.at[pl.ds(0, nxy - 1)], bsem.at[0])
    wait(back_ref.at[pl.ds(0, nxy - 1)], bsem.at[1])


def relay(pos, cid, by_z, meta, w_gate, w_up, w_down, cap):
    nx, ny, nz = pos.nx, pos.ny, pos.nz
    nxy = nx * ny
    _, depth, width = w_gate.shape
    tok, feats = by_z.shape
    piece = feats // nz
    lane = 128
    parts = width // lane
    rows = nz * cap
    wide = nx * lane
    dims = {"parts": parts, "rows": rows, "piece": piece, "top": 2, "depth": depth, "lane": lane}
    any_spec = pl.BlockSpec(memory_space=pl.ANY)
    vmem = pl.BlockSpec(memory_space=pltpu.VMEM)
    dma = pltpu.SemaphoreType.DMA
    return pl.pallas_call(
        lambda *refs: relay_kernel(pos, dims, refs),
        out_shape=[
            jax.ShapeDtypeStruct((nxy, rows, piece), BF16),
            jax.ShapeDtypeStruct((nz, *meta.shape), F32),
        ],
        in_specs=[vmem, vmem, any_spec, any_spec, any_spec],
        out_specs=[vmem, vmem],
        scratch_shapes=[
            pltpu.VMEM((nz, tok, piece), BF16),
            pltpu.VMEM((nxy, rows, piece), BF16),
            pltpu.VMEM((ny, rows, nx * piece), BF16),
            pltpu.VMEM((parts, 3, ny, 2, depth, wide), BF16),
            pltpu.VMEM((parts, nz, rows, 2 * wide), BF16),
            pltpu.VMEM((parts, 2, 2, nz // 2, rows, wide), BF16),
            pltpu.VMEM((parts, nz, rows, wide), BF16),
            pltpu.VMEM((nz, rows, ny * 2 * depth), F32),
            pltpu.VMEM((nz, rows, nx * piece), BF16),
            dma((2,)),
            dma((2,)),
            dma((12,)),
            dma((3, parts)),
            dma((3, parts)),
            dma((3, parts)),
            dma((3, parts)),
            dma,
            dma,
            dma((parts, 2, 2, nz // 2)),
            dma((parts, 2, 2, nz // 2)),
            dma((parts, 2, 2, nz // 2)),
            dma((parts, 2, 2, nz // 2)),
            dma((3,)),
        ],
        compiler_params=pltpu.CompilerParams(
            collective_id=cid, has_side_effects=True, vmem_limit_bytes=56 * 1024 * 1024
        ),
        name="relay",
    )(by_z, meta, w_gate, w_up, w_down)


def home_exchange(pos, cid, mixed):
    nz, tok, piece = mixed.shape

    def kernel(src, dst, sems):
        x, y, z, c = pos.here()
        signal_all(pos, x, y, z, c, pltpu.get_barrier_semaphore(), False, "all", False)
        cols = dst.at[:, pl.ds(pl.multiple_of(z * piece, piece), piece)]

        def body(k, carry):
            zz = lax.rem(z + k, nz)
            pltpu.make_async_remote_copy(
                src.at[zz], cols, sems.at[0], sems.at[1], device_id=pos.dev(x, y, zz, c), device_id_type=MESH
            ).start()
            return carry

        lax.fori_loop(1, nz, body, 0)
        own = pltpu.make_async_copy(src.at[z], cols, sems.at[2])
        own.start()
        own.wait()
        part = src.at[pl.ds(0, nz - 1)]
        pltpu.make_async_copy(part, part, sems.at[0]).wait()
        pltpu.make_async_copy(part, part, sems.at[1]).wait()

    vmem = pl.BlockSpec(memory_space=pltpu.VMEM)
    return pl.pallas_call(
        kernel,
        out_shape=jax.ShapeDtypeStruct((tok, nz * piece), mixed.dtype),
        in_specs=[vmem],
        out_specs=vmem,
        scratch_shapes=[pltpu.SemaphoreType.DMA((3,))],
        compiler_params=pltpu.CompilerParams(collective_id=cid, has_side_effects=True),
        name="home_exchange",
    )(mixed)


def shards(pos, tokens, routes, gate_prob, token_count, gate_weight, up_weight, down_weight):
    experts, depth, _ = gate_weight.shape
    nz, nzl = pos.nz, pos.nzl
    nzh = nz // nzl
    tok, feats = tokens.shape
    top = routes.shape[1]
    cap = min(tok, tok * top * 5 // (4 * experts))
    piece = feats // nz

    new = jnp.arange(feats, dtype=jnp.int32)
    zz, rest = new // piece, new % piece
    ylo, core, row = rest // (2 * depth), rest // depth % 2, rest % depth
    old = (((ylo * nzh + zz // nzl) * 2 + core) * nzl + zz % nzl) * depth + row
    shuffle = (jnp.arange(feats, dtype=jnp.int32)[:, None] == old[None, :]).astype(BF16)
    by_z = jnp.dot(tokens, shuffle, preferred_element_type=F32).astype(BF16)

    x, y, z, c = pos.here()
    positions = jnp.arange(tok, dtype=jnp.int32)
    live = positions < token_count[0]
    names = routes.T
    expert_ids = jnp.arange(experts, dtype=jnp.int32)
    named = [(expert_ids[:, None] == names[s][None, :]) & live[None, :] for s in range(top)]
    either = functools.reduce(jnp.logical_or, named).astype(BF16)
    earlier = (positions[:, None] < positions[None, :]).astype(BF16)
    rank = jnp.dot(either, earlier, preferred_element_type=F32).astype(jnp.int32)
    lines = []
    for s in range(top):
        place = (expert_ids[:, None] * nz + z) * cap + rank
        lines.append(jnp.sum(jnp.where(named[s], place + 1, 0), axis=0).astype(F32) - 1.0)
    lines += [gate_prob[:, s] for s in range(top)]
    meta = jnp.concatenate([jnp.stack(lines), jnp.zeros((8 - 2 * top, tok), F32)])

    back, infos = relay(pos, 1, by_z, meta, gate_weight, up_weight, down_weight, cap)

    slots_all = experts * nz * cap
    slot_of = [infos[:, s].astype(jnp.int32).reshape(nz * tok) for s in range(top)]
    slot_ids = jnp.arange(slots_all, dtype=jnp.int32)
    back = back.reshape(slots_all, piece)
    mixed = jnp.zeros((nz * tok, piece), F32)
    for s in range(top):
        chosen = (slot_of[s][:, None] == slot_ids[None, :]).astype(BF16)
        prob = infos[:, top + s].reshape(nz * tok)
        mixed = mixed + prob[:, None] * jnp.dot(chosen, back, preferred_element_type=F32)
    merged = home_exchange(pos, 2, mixed.astype(BF16).reshape(nz, tok, piece))
    unshuffle = (old[:, None] == jnp.arange(feats, dtype=jnp.int32)[None, :]).astype(BF16)
    return jnp.dot(merged, unshuffle, preferred_element_type=F32).astype(BF16)


def solution(mesh):
    nzl = mesh.shape["dp"]
    nx = mesh.shape["tensor"]
    nzh = 2
    ny = mesh.shape["expert"] // (2 * nzh)
    pos = Place(nx, ny, nzh * nzl, nzl)
    in_specs = (
        P(("expert", "dp"), "tensor"),
        P(("expert", "dp"), None),
        P(("expert", "dp"), None),
        P(("expert", "dp")),
        P(None, ("expert", "dp"), "tensor"),
        P(None, ("expert", "dp"), "tensor"),
        P(None, ("expert", "dp"), "tensor"),
    )
    out_specs = P(("expert", "dp"), "tensor")
    return jax.shard_map(
        functools.partial(shards, pos), mesh=mesh, in_specs=in_specs, out_specs=out_specs, check_vma=False
    )
```

```python
import functools

import jax
import jax.numpy as jnp
from jax import lax
from jax.experimental import pallas as pl
from jax.experimental.pallas import tpu as pltpu
from jax.sharding import PartitionSpec as P

MESH = pl.DeviceIdType.MESH
BF16 = jnp.bfloat16
F32 = jnp.float32


class Place:
    def __init__(self, nx, ny, nz, nzl):
        self.nx, self.ny, self.nz, self.nzl = nx, ny, nz, nzl
        self.nzh = nz // nzl

    def here(self):
        e = lax.axis_index("expert")
        x = lax.axis_index("tensor")
        zl = lax.axis_index("dp")
        core = lax.rem(e, 2)
        zh = lax.rem(e // 2, self.nzh)
        y = e // (2 * self.nzh)
        return x, y, zh * self.nzl + zl, core

    def dev(self, x, y, z, core):
        zh = z // self.nzl
        zl = lax.rem(z, self.nzl)
        return ((y * self.nzh + zh) * 2 + core, x, zl)


def signal_all(pos, x, y, z, c, barrier, xy, zring, core):
    n = 0
    if core:
        pl.semaphore_signal(barrier, inc=1, device_id=pos.dev(x, y, z, 1 - c), device_id_type=MESH)
        n += 1
    if zring == "ring":
        for dz in (1, pos.nz - 1):
            zz = lax.rem(z + dz, pos.nz)
            pl.semaphore_signal(barrier, inc=1, device_id=pos.dev(x, y, zz, c), device_id_type=MESH)
        n += 2
    if zring == "all":

        def zbody(k, carry):
            zz = lax.rem(z + k, pos.nz)
            pl.semaphore_signal(barrier, inc=1, device_id=pos.dev(x, y, zz, c), device_id_type=MESH)
            return carry

        lax.fori_loop(1, pos.nz, zbody, 0)
        n += pos.nz - 1
    if xy:

        def body(k, carry):
            xx = lax.rem(x + lax.rem(k, pos.nx), pos.nx)
            yy = lax.rem(y + k // pos.nx, pos.ny)
            pl.semaphore_signal(barrier, inc=1, device_id=pos.dev(xx, yy, z, c), device_id_type=MESH)
            return carry

        lax.fori_loop(1, pos.nx * pos.ny, body, 0)
        n += pos.nx * pos.ny - 1
    return n


def relay_kernel(pos, dims, refs):
    nx, ny, nz = pos.nx, pos.ny, pos.nz
    nxy = nx * ny
    parts, rows, piece, top = dims["parts"], dims["rows"], dims["piece"], dims["top"]
    depth, lane, tok, cap = dims["depth"], dims["lane"], dims["tok"], dims["cap"]
    feats = nz * piece
    half = nx * lane // 2
    (count_ref, tokens_ref, lines_ref, wg_ref, wu_ref, wd_ref, final_ref) = refs[:7]
    (tok_ref, meta_ref, perm, columns, info_ref, back_ref, back_wide, mixed, home) = refs[7:16]
    (raw, out_tok, x_in, wbuf, part, land, hid, acc, out) = refs[16:25]
    (zsend, zrecv, loc, wsend, wrecv, fsend, frecv, tsend, trecv, rsend, rrecv, asend, arecv, bsem, hsem) = refs[25:]
    me = pos.here()
    x, y, z, c = me
    weights = (wg_ref, wu_ref, wd_ref)
    partner = pos.dev(x, y, z, 1 - c)

    def remote(src, dst, s, r, dev):
        return pltpu.make_async_remote_copy(src, dst, s, r, device_id=dev, device_id_type=MESH)

    def wait(ref, sem):
        pltpu.make_async_copy(ref, ref, sem).wait()

    barrier = pltpu.get_barrier_semaphore()
    partners = signal_all(pos, x, y, z, c, barrier, True, "all", True)

    nzl = pos.nzl
    new = lax.broadcasted_iota(jnp.int32, (feats, 1), 0)
    at_z, rest = new // piece, lax.rem(new, piece)
    ylo, core, row = rest // (2 * depth), lax.rem(rest // depth, 2), lax.rem(rest, depth)
    old = (((ylo * pos.nzh + at_z // nzl) * 2 + core) * nzl + lax.rem(at_z, nzl)) * depth + row
    perm[...] = jnp.where(lax.broadcasted_iota(jnp.int32, (feats, feats), 1) == old, 1.0, 0.0).astype(BF16)
    tok_ref[...] = lax.dot_general(
        tokens_ref[...], perm[...], (((1,), (1,)), ((), ())), preferred_element_type=F32
    ).astype(BF16)

    experts = nxy
    expert_ids = lax.broadcasted_iota(jnp.int32, (experts, tok), 0).astype(F32)
    live = lax.broadcasted_iota(jnp.int32, (experts, tok), 1) < count_ref[0]
    named = [(expert_ids == lines_ref[s : s + 1, :]) & live for s in range(top)]
    either = jnp.where(functools.reduce(jnp.logical_or, named), 1.0, 0.0).astype(BF16)
    sooner = lax.broadcasted_iota(jnp.int32, (tok, tok), 0) < lax.broadcasted_iota(jnp.int32, (tok, tok), 1)
    rank = jnp.dot(either, jnp.where(sooner, 1.0, 0.0).astype(BF16), preferred_element_type=F32)
    meta_ref[...] = lines_ref[...]
    for s in range(top):
        place = jnp.where(named[s], expert_ids * cap + rank + 1.0, 0.0)
        meta_ref[s : s + 1, :] = jnp.sum(place, axis=0, keepdims=True) - 1.0

    pl.semaphore_wait(barrier, partners)

    def raw_send(k, carry):
        zz = lax.rem(z + k, nz)
        dev = pos.dev(x, y, zz, c)
        cols = pl.ds(pl.multiple_of(zz * piece, piece), piece)
        remote(meta_ref, info_ref.at[z], zsend.at[1], zrecv.at[1], dev).start()
        remote(tok_ref.at[:, cols], raw.at[z], zsend.at[0], zrecv.at[0], dev).start()
        return carry

    lax.fori_loop(1, nz, raw_send, 0)
    own_cols = pl.ds(pl.multiple_of(z * piece, piece), piece)
    own_raw = pltpu.make_async_copy(tok_ref.at[:, own_cols], raw.at[z], loc.at[0])
    own_meta = pltpu.make_async_copy(meta_ref, info_ref.at[z], loc.at[1])
    own_raw.start()
    own_meta.start()

    def w_src(m, w, e):
        return weights[m].at[e, :, pl.ds(w * lane, lane)]

    def w_dst(m, w, xs, ys, cs):
        return wbuf.at[w, m, ys, cs, :, pl.ds(pl.multiple_of(xs * lane, lane), lane)]

    def w_start(w, mats):
        def body(k, carry):
            xx = lax.rem(x + lax.rem(k, nx), nx)
            yy = lax.rem(y + k // nx, ny)
            dev = pos.dev(xx, yy, z, c)
            for m in mats:
                remote(w_src(m, w, yy * nx + xx), w_dst(m, w, x, y, c), wsend.at[m, w], wrecv.at[m, w], dev).start()
            return carry

        lax.fori_loop(1, nxy, body, 0)
        for m in mats:
            pltpu.make_async_copy(w_src(m, w, y * nx + x), w_dst(m, w, x, y, c), loc.at[2 + 3 * w + m]).start()

    def w_forward(w, mats):
        for m in mats:
            pltpu.make_async_copy(w_src(m, w, y * nx + x), w_dst(m, w, x, y, c), loc.at[2 + 3 * w + m]).wait()
            wait(weights[m].at[pl.ds(0, nxy - 1), :, pl.ds(w * lane, lane)], wrecv.at[m, w])
            block = wbuf.at[w, m, :, c]
            remote(block, block, fsend.at[m, w], frecv.at[m, w], partner).start()

    def w_ready(w, mats):
        for m in mats:
            wait(wbuf.at[w, m, :, 0], frecv.at[m, w])

    w_start(0, (0, 1))

    own_raw.wait()
    own_meta.wait()
    for i, ref in ((1, info_ref), (0, raw)):
        wait(ref.at[pl.ds(0, nz - 1)], zsend.at[i])
        wait(ref.at[pl.ds(0, nz - 1)], zrecv.at[i])
    count = nx * rows

    def dispatch(dy):
        yy = lax.rem(y + dy, ny)
        ids = lax.broadcasted_iota(jnp.int32, (count, raw.shape[1]), 0).astype(F32)
        base = (yy * count).astype(F32)
        picks = []
        for zz in range(nz):
            hit = None
            for s in range(top):
                same = ids == (info_ref[zz, s : s + 1, :] * nz + (zz - base))
                hit = same if hit is None else hit | same
            picks.append(jnp.where(hit, 1.0, 0.0).astype(BF16))
        pick = jnp.concatenate(picks, axis=1)
        feats = raw[...].reshape(nz * raw.shape[1], piece)
        got = jnp.dot(pick, feats, preferred_element_type=F32).astype(BF16)
        out_tok[pl.ds(yy * nx, nx)] = got.reshape(nx, rows, piece)

    def t_dst(xs, ys):
        return x_in.at[ys, :, pl.ds(pl.multiple_of(xs * piece, piece), piece)]

    def t_send(dy, first):
        yy = lax.rem(y + dy, ny)
        for dx in range(first, nx):
            xx = lax.rem(x + dx, nx)
            remote(out_tok.at[yy * nx + xx], t_dst(x, y), tsend, trecv, pos.dev(xx, yy, z, c)).start()

    dispatch(1)

    def d_body(dy, carry):
        dispatch(dy)
        t_send(dy - 1, 0)
        return carry

    lax.fori_loop(2, ny, d_body, 0)
    dispatch(0)
    t_send(ny - 1, 0)
    w_start(1, (0, 1))
    t_send(0, 1)
    own_tok = pltpu.make_async_copy(out_tok.at[y * nx + x], t_dst(x, y), loc.at[11])
    own_tok.start()
    w_forward(0, (0, 1))

    for zz in range(nz):
        columns[zz] = jnp.transpose(info_ref[zz])

    def product(w):
        wide = nx * lane
        for m in range(2):
            right = wbuf[w, m].reshape(ny * 2 * depth, wide)

            def body(i, carry):
                left = x_in[pl.ds(i * (ny // 2), ny // 2)].reshape(ny // 2 * rows, nx * piece)
                res = jnp.dot(left, right, preferred_element_type=F32).astype(BF16)
                part[w, pl.ds(i * (ny // 2), ny // 2), :, m * wide : (m + 1) * wide] = res.reshape(ny // 2, rows, wide)
                return carry

            lax.fori_loop(0, 2, body, 0)

    step = (1, nz - 1)
    near = (pos.dev(x, y, lax.rem(z + 1, nz), c), pos.dev(x, y, lax.rem(z + nz - 1, nz), c))
    far = nz // 2
    chains = [(d, h, far if h == d else far - 1) for h in range(2) for d in range(2)]
    wide = nx * lane

    def at(d, k):
        return lax.rem(z + (k if d == 0 else -k) + 2 * nz, nz)

    def rs_send(w, d, h, i, src):
        remote(src, land.at[w, d, h, i], rsend.at[w, d, h, i], rrecv.at[w, d, h, i], near[d]).start()

    def rs_start(w):
        for d, h, n in chains:
            rs_send(w, d, h, 0, part.at[w, at(d, n), :, pl.ds(h * wide, wide)])

    def rs_mid(w, i):
        for d, h, n in chains:
            if i < n:
                slot = land.at[w, d, h, i - 1]
                wait(slot, rrecv.at[w, d, h, i - 1])
                mine = part[w, at(d, n - i), :, pl.ds(h * wide, wide)]
                slot[...] = (slot[...].astype(F32) + mine.astype(F32)).astype(BF16)
        for d, h, n in chains:
            if i < n:
                rs_send(w, d, h, i, land.at[w, d, h, i - 1])

    def ag_send(w, d, h, i, j):
        block = hid.at[w, j, :, pl.ds(h * half, half)]
        remote(block, block, asend.at[w, d, h, i], arecv.at[w, d, h, i], near[d]).start()

    def rs_final(w):
        total = []
        for h in range(2):
            t = part[w, z, :, pl.ds(h * wide, wide)].astype(F32)
            for d, hh, n in chains:
                if hh == h:
                    slot = land.at[w, d, h, n - 1]
                    wait(slot, rrecv.at[w, d, h, n - 1])
                    t = t + slot[...].astype(F32)
            total.append(t)
        gate, up = total
        hid[w, z] = (gate / (1.0 + jnp.exp(-gate)) * up).astype(BF16)

    def ag_start(w):
        for d, h, n in chains:
            ag_send(w, d, h, 0, z)

    def ag_mid(w, i):
        for d, h, n in chains:
            if i <= n:
                j = at(d, -i)
                wait(hid.at[w, j, :, pl.ds(h * half, half)], arecv.at[w, d, h, i - 1])
                if i < n:
                    ag_send(w, d, h, i, j)

    def down(w, left):
        return lax.dot_general(
            left, wbuf[w, 2].reshape(ny * 2 * depth, wide), (((1,), (1,)), ((), ())), preferred_element_type=F32
        )

    def accumulate(w):
        def body(i, carry):
            span = pl.ds(i * (nz // 2), nz // 2)
            res = down(w, hid[w, span].reshape(nz // 2 * rows, wide)).reshape(nz // 2, rows, ny * 2 * depth)
            acc[span] = res if w == 0 else acc[span] + res
            return carry

        lax.fori_loop(0, 2, body, 0)

    def o_src(xx, j):
        return out.at[j, :, pl.ds(pl.multiple_of(xx * piece, piece), piece)]

    def finish_rows(js):
        last = parts - 1
        left = jnp.concatenate([hid[last, j] for j in js], axis=0) if len(js) > 1 else hid[last, js[0]]
        res = down(last, left)
        for i, j in enumerate(js):
            out[j] = (acc[j] + res[i * rows : (i + 1) * rows]).astype(BF16)

    def send_rows(js):
        for j in js:
            for dx in range(nx):
                xx = lax.rem(x + dx, nx)
                away = remote(o_src(xx, j), back_ref.at[y * nx + x], bsem.at[0], bsem.at[1], pos.dev(xx, j, z, c))
                if dx:
                    away.start()
                else:

                    @pl.when(j != y)
                    def _():
                        away.start()

                    @pl.when(j == y)
                    def _():
                        pltpu.make_async_copy(o_src(x, y), back_ref.at[y * nx + x], bsem.at[2]).start()

    own_tok.wait()
    wait(out_tok.at[pl.ds(0, nxy - 1)], tsend)
    wait(out_tok.at[pl.ds(0, nxy - 1)], trecv)
    w_ready(0, (0, 1))
    product(0)
    rs_start(0)
    w_start(2, (0, 1))
    rs_mid(0, 1)
    w_forward(1, (0, 1))
    rs_mid(0, 2)
    w_ready(1, (0, 1))
    product(1)
    rs_start(1)
    for w in range(parts):
        w_start(w, (2,))
    rs_mid(0, 3)
    rs_mid(1, 1)
    rs_final(0)
    w_forward(2, (0, 1))
    ag_start(0)
    rs_mid(1, 2)
    w_ready(2, (0, 1))
    product(2)
    rs_start(2)
    ag_mid(0, 1)
    rs_mid(1, 3)
    rs_mid(2, 1)
    ag_mid(0, 2)
    rs_final(1)
    ag_start(1)
    rs_mid(2, 2)
    ag_mid(0, 3)
    ag_mid(1, 1)
    w_forward(0, (2,))
    rs_mid(2, 3)
    ag_mid(0, 4)
    ag_mid(1, 2)
    w_ready(0, (2,))
    accumulate(0)
    rs_final(2)
    w_forward(1, (2,))
    ag_start(2)
    ag_mid(1, 3)
    w_forward(2, (2,))
    ag_mid(1, 4)
    w_ready(1, (2,))
    w_ready(2, (2,))
    ag_mid(2, 1)
    accumulate(1)
    finish_rows([z])
    ag_mid(2, 2)
    finish_rows([at(0, 1), at(1, 1)])
    send_rows([z])
    ag_mid(2, 3)
    finish_rows([at(0, 2), at(1, 2)])
    send_rows([at(0, 1), at(1, 1)])
    ag_mid(2, 4)
    finish_rows([at(0, 3), at(1, 3)])
    send_rows([at(0, 2), at(1, 2)])
    finish_rows([at(0, 4)])
    send_rows([at(0, 3), at(1, 3), at(0, 4)])

    pltpu.make_async_copy(o_src(x, y), back_ref.at[y * nx + x], bsem.at[2]).wait()
    wait(back_ref.at[pl.ds(0, nxy - 1)], bsem.at[1])
    back_wide[...] = back_ref[...].reshape(nxy * rows, piece).astype(F32)
    slots = experts * cap
    slot_ids = lax.broadcasted_iota(jnp.int32, (tok, slots), 1).astype(F32)

    def combine(k):
        zz = lax.rem(z + k, nz)
        mine = back_wide[pl.ds(zz, slots, stride=nz), :].astype(BF16)
        cols = columns[zz]
        total = jnp.zeros((tok, piece), F32)
        for s in range(top):
            chosen = jnp.where(slot_ids == cols[:, s : s + 1], 1.0, 0.0).astype(BF16)
            total = total + cols[:, top + s : top + s + 1] * jnp.dot(chosen, mine, preferred_element_type=F32)
        mixed[zz] = total.astype(BF16)

    def home_send(k):
        zz = lax.rem(z + k, nz)
        remote(mixed.at[zz], home.at[z], hsem.at[0], hsem.at[1], pos.dev(x, y, zz, c)).start()

    combine(1)

    def home_body(k, carry):
        combine(k)
        home_send(k - 1)
        return carry

    lax.fori_loop(2, nz, home_body, 0)
    combine(0)
    home_send(nz - 1)
    own_home = pltpu.make_async_copy(mixed.at[z], home.at[z], hsem.at[2])
    own_home.start()

    for m in range(3):
        for w in range(parts):
            wait(weights[m].at[pl.ds(0, nxy - 1), :, pl.ds(w * lane, lane)], wsend.at[m, w])
            wait(wbuf.at[w, m, :, 0], fsend.at[m, w])
    for w in range(parts):
        for d, h, n in chains:
            for i in range(n):
                wait(land.at[w, d, h, i], rsend.at[w, d, h, i])
                wait(hid.at[w, z, :, pl.ds(h * half, half)], asend.at[w, d, h, i])
    wait(back_ref.at[pl.ds(0, nxy - 1)], bsem.at[0])
    own_home.wait()
    wait(mixed.at[pl.ds(0, nz - 1)], hsem.at[0])
    wait(home.at[pl.ds(0, nz - 1)], hsem.at[1])
    merged = jnp.concatenate([home[i] for i in range(nz)], axis=1)
    final_ref[...] = jnp.dot(merged, perm[...], preferred_element_type=F32).astype(BF16)


def relay(pos, cid, token_count, tokens, lines, w_gate, w_up, w_down, cap):
    nx, ny, nz = pos.nx, pos.ny, pos.nz
    nxy = nx * ny
    _, depth, width = w_gate.shape
    tok, feats = tokens.shape
    piece = feats // nz
    lane = 128
    parts = width // lane
    rows = nz * cap
    wide = nx * lane
    dims = {
        "parts": parts, "rows": rows, "piece": piece, "top": 2, "depth": depth, "lane": lane, "tok": tok, "cap": cap
    }
    any_spec = pl.BlockSpec(memory_space=pl.ANY)
    vmem = pl.BlockSpec(memory_space=pltpu.VMEM)
    smem = pl.BlockSpec(memory_space=pltpu.SMEM)
    dma = pltpu.SemaphoreType.DMA
    return pl.pallas_call(
        lambda *refs: relay_kernel(pos, dims, refs),
        out_shape=jax.ShapeDtypeStruct((tok, feats), BF16),
        in_specs=[smem, vmem, vmem, any_spec, any_spec, any_spec],
        out_specs=vmem,
        scratch_shapes=[
            pltpu.VMEM((tok, feats), BF16),
            pltpu.VMEM((8, tok), F32),
            pltpu.VMEM((feats, feats), BF16),
            pltpu.VMEM((nz, tok, 8), F32),
            pltpu.VMEM((nz, 8, tok), F32),
            pltpu.VMEM((nxy, rows, piece), BF16),
            pltpu.VMEM((nxy * rows, piece), F32),
            pltpu.VMEM((nz, tok, piece), BF16),
            pltpu.VMEM((nz, tok, piece), BF16),
            pltpu.VMEM((nz, tok, piece), BF16),
            pltpu.VMEM((nxy, rows, piece), BF16),
            pltpu.VMEM((ny, rows, nx * piece), BF16),
            pltpu.VMEM((parts, 3, ny, 2, depth, wide), BF16),
            pltpu.VMEM((parts, nz, rows, 2 * wide), BF16),
            pltpu.VMEM((parts, 2, 2, nz // 2, rows, wide), BF16),
            pltpu.VMEM((parts, nz, rows, wide), BF16),
            pltpu.VMEM((nz, rows, ny * 2 * depth), F32),
            pltpu.VMEM((nz, rows, nx * piece), BF16),
            dma((2,)),
            dma((2,)),
            dma((12,)),
            dma((3, parts)),
            dma((3, parts)),
            dma((3, parts)),
            dma((3, parts)),
            dma,
            dma,
            dma((parts, 2, 2, nz // 2)),
            dma((parts, 2, 2, nz // 2)),
            dma((parts, 2, 2, nz // 2)),
            dma((parts, 2, 2, nz // 2)),
            dma((3,)),
            dma((3,)),
        ],
        compiler_params=pltpu.CompilerParams(
            collective_id=cid, has_side_effects=True, vmem_limit_bytes=56 * 1024 * 1024
        ),
        name="relay",
    )(token_count, tokens, lines, w_gate, w_up, w_down)


def shards(pos, tokens, routes, gate_prob, token_count, gate_weight, up_weight, down_weight):
    experts = gate_weight.shape[0]
    tok, top = routes.shape
    cap = min(tok, tok * top * 5 // (4 * experts))
    lines = jnp.concatenate([routes.astype(F32), gate_prob, jnp.zeros((tok, 8 - 2 * top), F32)], axis=1).T
    return relay(pos, 1, token_count, tokens, lines, gate_weight, up_weight, down_weight, cap)


def solution(mesh):
    nzl = mesh.shape["dp"]
    nx = mesh.shape["tensor"]
    nzh = 2
    ny = mesh.shape["expert"] // (2 * nzh)
    pos = Place(nx, ny, nzh * nzl, nzl)
    in_specs = (
        P(("expert", "dp"), "tensor"),
        P(("expert", "dp"), None),
        P(("expert", "dp"), None),
        P(("expert", "dp")),
        P(None, ("expert", "dp"), "tensor"),
        P(None, ("expert", "dp"), "tensor"),
        P(None, ("expert", "dp"), "tensor"),
    )
    out_specs = P(("expert", "dp"), "tensor")
    return jax.shard_map(
        functools.partial(shards, pos), mesh=mesh, in_specs=in_specs, out_specs=out_specs, check_vma=False
    )
```

```python
import functools

import jax
import jax.numpy as jnp
from jax import lax
from jax.experimental import pallas as pl
from jax.experimental.pallas import tpu as pltpu
from jax.sharding import PartitionSpec as P

MESH = pl.DeviceIdType.MESH
BF16 = jnp.bfloat16
F32 = jnp.float32


class Place:
    def __init__(self, nx, ny, nz, nzl):
        self.nx, self.ny, self.nz, self.nzl = nx, ny, nz, nzl
        self.nzh = nz // nzl

    def here(self):
        e = lax.axis_index("expert")
        x = lax.axis_index("tensor")
        zl = lax.axis_index("dp")
        core = lax.rem(e, 2)
        zh = lax.rem(e // 2, self.nzh)
        y = e // (2 * self.nzh)
        return x, y, zh * self.nzl + zl, core

    def dev(self, x, y, z, core):
        zh = z // self.nzl
        zl = lax.rem(z, self.nzl)
        return ((y * self.nzh + zh) * 2 + core, x, zl)


def signal_all(pos, x, y, z, c, barrier, xy, zring, core):
    n = 0
    if core:
        pl.semaphore_signal(barrier, inc=1, device_id=pos.dev(x, y, z, 1 - c), device_id_type=MESH)
        n += 1
    if zring == "ring":
        for dz in (1, pos.nz - 1):
            zz = lax.rem(z + dz, pos.nz)
            pl.semaphore_signal(barrier, inc=1, device_id=pos.dev(x, y, zz, c), device_id_type=MESH)
        n += 2
    if zring == "all":

        def zbody(k, carry):
            zz = lax.rem(z + k, pos.nz)
            pl.semaphore_signal(barrier, inc=1, device_id=pos.dev(x, y, zz, c), device_id_type=MESH)
            return carry

        lax.fori_loop(1, pos.nz, zbody, 0)
        n += pos.nz - 1
    if xy:

        def body(k, carry):
            xx = lax.rem(x + lax.rem(k, pos.nx), pos.nx)
            yy = lax.rem(y + k // pos.nx, pos.ny)
            pl.semaphore_signal(barrier, inc=1, device_id=pos.dev(xx, yy, z, c), device_id_type=MESH)
            return carry

        lax.fori_loop(1, pos.nx * pos.ny, body, 0)
        n += pos.nx * pos.ny - 1
    return n


def relay_kernel(pos, dims, refs):
    nx, ny, nz = pos.nx, pos.ny, pos.nz
    nxy = nx * ny
    parts, rows, piece, top = dims["parts"], dims["rows"], dims["piece"], dims["top"]
    depth, lane, tok, cap = dims["depth"], dims["lane"], dims["tok"], dims["cap"]
    feats = nz * piece
    half = nx * lane // 2
    (count_ref, tokens_ref, names_ref, prob_ref, wg_ref, wu_ref, wd_ref, final_ref) = refs[:8]
    (tok_ref, meta_ref, perm, columns, info_ref, back_ref, back_wide, mixed, home) = refs[8:17]
    (raw, out_tok, x_in, wbuf, part, land, hid, perm_back, out) = refs[17:26]
    (zsend, zrecv, loc, wsend, wrecv, fsend, frecv, tsend, trecv, rsend, rrecv, asend, arecv, bsem, hsem) = refs[26:]
    me = pos.here()
    x, y, z, c = me
    weights = (wg_ref, wu_ref, wd_ref)
    partner = pos.dev(x, y, z, 1 - c)

    def remote(src, dst, s, r, dev):
        return pltpu.make_async_remote_copy(src, dst, s, r, device_id=dev, device_id_type=MESH)

    def wait(ref, sem):
        pltpu.make_async_copy(ref, ref, sem).wait()

    barrier = pltpu.get_barrier_semaphore()
    partners = signal_all(pos, x, y, z, c, barrier, True, "all", True)

    nzl, nzh = pos.nzl, pos.nzh
    nseg = piece // depth
    block = nzl * depth
    lanes = lax.broadcasted_iota(jnp.int32, (1, nzl * piece), 1)
    inner = lax.rem(lanes, piece)
    source = (inner // depth) * block + (lanes // piece) * depth + lax.rem(inner, depth)
    ids = lax.broadcasted_iota(jnp.int32, (nseg * block, nzl * piece), 0)
    perm[...] = jnp.where(ids == source, 1.0, 0.0).astype(BF16)

    def blocks_of(zh):
        return [pl.ds((((seg // 2) * nzh + zh) * 2 + seg % 2) * block, block) for seg in range(nseg)]

    for zh in range(nzh):
        left = jnp.concatenate([tokens_ref[:, b] for b in blocks_of(zh)], axis=1)
        got = jnp.dot(left, perm[...], preferred_element_type=F32).astype(BF16)
        for zl in range(nzl):
            tok_ref[zh * nzl + zl] = got[:, zl * piece : (zl + 1) * piece]

    experts = nxy
    expert_ids = lax.broadcasted_iota(jnp.int32, (experts, tok), 0)
    live = lax.broadcasted_iota(jnp.int32, (experts, tok), 1) < count_ref[0]
    named = [(expert_ids == names_ref[s : s + 1, :]) & live for s in range(top)]
    either = jnp.where(functools.reduce(jnp.logical_or, named), 1.0, 0.0).astype(BF16)
    sooner = lax.broadcasted_iota(jnp.int32, (tok, tok), 0) < lax.broadcasted_iota(jnp.int32, (tok, tok), 1)
    rank = jnp.dot(either, jnp.where(sooner, 1.0, 0.0).astype(BF16), preferred_element_type=F32)
    meta_ref[...] = jnp.zeros_like(meta_ref)
    meta_ref[top : 2 * top, :] = prob_ref[...]
    for s in range(top):
        place = jnp.where(named[s], (expert_ids * cap).astype(F32) + rank + 1.0, 0.0)
        meta_ref[s : s + 1, :] = jnp.sum(place, axis=0, keepdims=True) - 1.0

    pl.semaphore_wait(barrier, partners)

    def far_first(i):
        return nz // 2 + (1 - 2 * lax.rem(i, 2)) * ((i + 1) // 2)

    def raw_send(i, carry):
        zz = lax.rem(z + far_first(i), nz)
        dev = pos.dev(x, y, zz, c)
        remote(tok_ref.at[zz], raw.at[z], zsend.at[0], zrecv.at[0], dev).start()
        remote(meta_ref, info_ref.at[z], zsend.at[1], zrecv.at[1], dev).start()
        return carry

    lax.fori_loop(0, nz - 1, raw_send, 0)
    own_raw = pltpu.make_async_copy(tok_ref.at[z], raw.at[z], loc.at[0])
    own_meta = pltpu.make_async_copy(meta_ref, info_ref.at[z], loc.at[1])
    own_raw.start()
    own_meta.start()

    def w_src(m, w, e):
        return weights[m].at[e, :, pl.ds(w * lane, lane)]

    def w_dst(m, w, xs, ys, cs):
        return wbuf.at[w, m, ys, cs, :, pl.ds(pl.multiple_of(xs * lane, lane), lane)]

    def w_start(w, mats):
        def body(k, carry):
            xx = lax.rem(x + lax.rem(k, nx), nx)
            yy = lax.rem(y + k // nx, ny)
            dev = pos.dev(xx, yy, z, c)
            for m in mats:
                remote(w_src(m, w, yy * nx + xx), w_dst(m, w, x, y, c), wsend.at[m, w], wrecv.at[m, w], dev).start()
            return carry

        lax.fori_loop(1, nxy, body, 0)
        for m in mats:
            pltpu.make_async_copy(w_src(m, w, y * nx + x), w_dst(m, w, x, y, c), loc.at[2 + 3 * w + m]).start()

    def w_forward(w, mats):
        for m in mats:
            pltpu.make_async_copy(w_src(m, w, y * nx + x), w_dst(m, w, x, y, c), loc.at[2 + 3 * w + m]).wait()
            wait(weights[m].at[pl.ds(0, nxy - 1), :, pl.ds(w * lane, lane)], wrecv.at[m, w])
            block = wbuf.at[w, m, :, c]
            remote(block, block, fsend.at[m, w], frecv.at[m, w], partner).start()

    def w_ready(w, mats):
        for m in mats:
            wait(wbuf.at[w, m, :, 0], frecv.at[m, w])

    w_start(0, (0, 1))

    own_raw.wait()
    own_meta.wait()
    for i, ref in ((1, info_ref), (0, raw)):
        wait(ref.at[pl.ds(0, nz - 1)], zsend.at[i])
        wait(ref.at[pl.ds(0, nz - 1)], zrecv.at[i])
    count = nx * rows

    def dy_of(i):
        return lax.rem(3 * nz - z - far_first(i), nz)

    def dispatch(i):
        yy = lax.rem(y + dy_of(i), ny)
        ids = lax.broadcasted_iota(jnp.int32, (count, raw.shape[1]), 0).astype(F32)
        base = (yy * count).astype(F32)
        picks = []
        for zz in range(nz):
            hit = None
            for s in range(top):
                same = ids == (info_ref[zz, s : s + 1, :] * nz + (zz - base))
                hit = same if hit is None else hit | same
            picks.append(jnp.where(hit, 1.0, 0.0).astype(BF16))
        pick = jnp.concatenate(picks, axis=1)
        got = jnp.dot(pick, raw[...].reshape(nz * tok, piece), preferred_element_type=F32).astype(BF16)
        out_tok[pl.ds(yy * nx, nx)] = got.reshape(nx, rows, piece)

    def t_dst(xs, ys):
        return x_in.at[ys, :, pl.ds(pl.multiple_of(xs * piece, piece), piece)]

    def t_send(i):
        dy = dy_of(i)
        yy = lax.rem(y + dy, ny)
        for dx in range(nx):
            xx = lax.rem(x + dx, nx)
            away = remote(out_tok.at[yy * nx + xx], t_dst(x, y), tsend.at[i], trecv.at[dy], pos.dev(xx, yy, z, c))
            if dx:
                away.start()
            else:

                @pl.when(dy != 0)
                def _():
                    away.start()

                @pl.when(dy == 0)
                def _():
                    pltpu.make_async_copy(out_tok.at[y * nx + x], t_dst(x, y), loc.at[11]).start()

    def t_sent(i):
        dy = dy_of(i)

        @pl.when(dy == 0)
        def _():
            wait(out_tok.at[pl.ds(0, nx - 1)], tsend.at[i])

        @pl.when(dy != 0)
        def _():
            wait(out_tok.at[pl.ds(0, nx)], tsend.at[i])

    dispatch(0)

    def d_body(i, carry):
        dispatch(i)
        t_send(i - 1)
        return carry

    lax.fori_loop(1, 5, d_body, 0)

    def d_late(i, carry):
        dispatch(i)
        t_sent(i - 5)
        t_send(i - 1)
        return carry

    lax.fori_loop(5, ny, d_late, 0)
    for zz in range(nz):
        columns[zz] = jnp.transpose(info_ref[zz])
    lanes = lax.broadcasted_iota(jnp.int32, (1, nseg * block), 1)
    inner = lax.rem(lanes, block)
    source = (inner // depth) * piece + (lanes // block) * depth + lax.rem(inner, depth)
    ids = lax.broadcasted_iota(jnp.int32, (nzl * piece, nseg * block), 0)
    perm_back[...] = jnp.where(ids == source, 1.0, 0.0).astype(BF16)
    t_sent(3)
    t_send(ny - 1)
    w_forward(0, (0, 1))
    t_sent(4)
    t_sent(5)
    w_start(1, (0, 1))

    def token_wait(i):
        dy = dy_of(i)

        @pl.when(dy == 0)
        def _():
            pltpu.make_async_copy(out_tok.at[y * nx + x], t_dst(x, y), loc.at[11]).wait()
            wait(x_in.at[0, :, pl.ds(0, (nx - 1) * piece)], trecv.at[0])

        @pl.when(dy != 0)
        def _():
            wait(x_in.at[0], trecv.at[dy])

    def first_part(order):
        js = [lax.rem(z + y + far_first(i), nz) for i in order]
        left = jnp.concatenate([x_in[j] for j in js], axis=0) if len(js) > 1 else x_in[js[0]]
        for m in range(2):
            res = jnp.dot(left, wbuf[0, m].reshape(ny * 2 * depth, nx * lane), preferred_element_type=F32).astype(BF16)
            for i, j in enumerate(js):
                part[0, j, :, m * nx * lane : (m + 1) * nx * lane] = res[i * rows : (i + 1) * rows]

    def product(w):
        wide = nx * lane
        for m in range(2):
            right = wbuf[w, m].reshape(ny * 2 * depth, wide)

            def body(i, carry):
                left = x_in[pl.ds(i * (ny // 2), ny // 2)].reshape(ny // 2 * rows, nx * piece)
                res = jnp.dot(left, right, preferred_element_type=F32).astype(BF16)
                part[w, pl.ds(i * (ny // 2), ny // 2), :, m * wide : (m + 1) * wide] = res.reshape(ny // 2, rows, wide)
                return carry

            lax.fori_loop(0, 2, body, 0)

    step = (1, nz - 1)
    near = (pos.dev(x, y, lax.rem(z + 1, nz), c), pos.dev(x, y, lax.rem(z + nz - 1, nz), c))
    far = nz // 2
    chains = [(d, h, far if h == d else far - 1) for h in range(2) for d in range(2)]
    wide = nx * lane

    mine_at = lax.rem(z + y, nz)

    def at(d, k):
        return lax.rem(mine_at + (k if d == 0 else -k) + 2 * nz, nz)

    def rs_send(w, d, h, i, src):
        remote(src, land.at[w, d, h, i], rsend.at[w, d, h, i], rrecv.at[w, d, h, i], near[d]).start()

    def rs_start(w):
        for d, h, n in chains:
            rs_send(w, d, h, 0, part.at[w, at(d, n), :, pl.ds(h * wide, wide)])

    def rs_mid(w, i):
        ready = None
        for d, h, n in chains:
            if i < n:
                slot = land.at[w, d, h, i - 1]
                wait(slot, rrecv.at[w, d, h, i - 1])
                mine = part[w, at(d, n - i), :, pl.ds(h * wide, wide)]
                slot[...] = (slot[...].astype(F32) + mine.astype(F32)).astype(BF16)
                if ready is not None:
                    rs_send(w, *ready)
                ready = (d, h, i, slot)
        if ready is not None:
            rs_send(w, *ready)

    cuts = ((0, 48), (48, rows - 48))

    def hid_cut(w, j, h, p):
        return hid.at[w, j, pl.ds(*cuts[p]), pl.ds(h * half, half)]

    def ag_send(w, d, h, i, j, p):
        block = hid_cut(w, j, h, p)
        remote(block, block, asend.at[w, d, h, i, p], arecv.at[w, d, h, i, p], near[d]).start()

    def rs_final(w):
        total = []
        for h in range(2):
            t = part[w, mine_at, :, pl.ds(h * wide, wide)].astype(F32)
            for d, hh, n in chains:
                if hh == h:
                    slot = land.at[w, d, h, n - 1]
                    wait(slot, rrecv.at[w, d, h, n - 1])
                    t = t + slot[...].astype(F32)
            total.append(t)
        gate, up = total
        hid[w, mine_at] = (gate / (1.0 + jnp.exp(-gate)) * up).astype(BF16)

    def ag_start(w):
        for p in range(len(cuts)):
            for d, h, n in chains:
                ag_send(w, d, h, 0, mine_at, p)

    def ag_mid(w, i):
        for p in range(len(cuts)):
            for d, h, n in chains:
                if i <= n:
                    j = at(d, -i)
                    wait(hid_cut(w, j, h, p), arecv.at[w, d, h, i - 1, p])
                    if i < n:
                        ag_send(w, d, h, i, j, p)

    def o_src(xx, j):
        return out.at[j, :, pl.ds(pl.multiple_of(xx * piece, piece), piece)]

    def finish_rows(js):
        res = None
        for w in range(parts):
            left = jnp.concatenate([hid[w, j] for j in js], axis=0) if len(js) > 1 else hid[w, js[0]]
            right = wbuf[w, 2].reshape(ny * 2 * depth, wide)
            more = lax.dot_general(left, right, (((1,), (1,)), ((), ())), preferred_element_type=F32)
            res = more if res is None else res + more
        for i, j in enumerate(js):
            out[j] = res[i * rows : (i + 1) * rows].astype(BF16)

    def send_rows(js):
        for j in js:
            for dx in range(nx):
                xx = lax.rem(x + dx, nx)
                away = remote(o_src(xx, j), back_ref.at[y * nx + x], bsem.at[0], bsem.at[1], pos.dev(xx, j, z, c))
                if dx:
                    away.start()
                else:

                    @pl.when(j != y)
                    def _():
                        away.start()

                    @pl.when(j == y)
                    def _():
                        pltpu.make_async_copy(o_src(x, y), back_ref.at[y * nx + x], bsem.at[2]).start()

    w_ready(0, (0, 1))
    token_wait(0)
    token_wait(1)
    token_wait(2)
    first_part([0])
    first_part([1, 2])
    rs_start(0)
    token_wait(3)
    token_wait(4)
    first_part([3, 4])
    rs_mid(0, 1)
    token_wait(5)
    token_wait(6)
    first_part([5, 6])
    token_wait(7)
    first_part([7])
    w_start(2, (0, 1))
    rs_mid(0, 2)
    w_forward(1, (0, 1))
    rs_mid(0, 3)
    w_ready(1, (0, 1))
    product(1)
    rs_start(1)
    for w in range(parts):
        w_start(w, (2,))
    rs_final(0)
    ag_start(0)
    rs_mid(1, 1)
    w_forward(2, (0, 1))
    rs_mid(1, 2)
    w_ready(2, (0, 1))
    product(2)
    rs_start(2)
    ag_mid(0, 1)
    rs_mid(1, 3)
    rs_mid(2, 1)
    ag_mid(0, 2)
    rs_final(1)
    ag_start(1)
    rs_mid(2, 2)
    ag_mid(0, 3)
    ag_mid(1, 1)
    w_forward(0, (2,))
    rs_mid(2, 3)
    ag_mid(0, 4)
    ag_mid(1, 2)
    w_forward(1, (2,))
    w_forward(2, (2,))
    w_ready(0, (2,))
    rs_final(2)
    ag_start(2)
    w_ready(1, (2,))
    w_ready(2, (2,))
    finish_rows([mine_at])
    send_rows([mine_at])
    ag_mid(1, 3)
    ag_mid(2, 1)
    finish_rows([at(0, 1), at(1, 1)])
    send_rows([at(0, 1), at(1, 1)])
    ag_mid(1, 4)
    ag_mid(2, 2)
    finish_rows([at(0, 2), at(1, 2)])
    send_rows([at(0, 2), at(1, 2)])
    ag_mid(2, 3)
    finish_rows([at(0, 3), at(1, 3)])
    send_rows([at(0, 3), at(1, 3)])
    ag_mid(2, 4)
    finish_rows([at(0, 4)])
    send_rows([at(0, 4)])

    pltpu.make_async_copy(o_src(x, y), back_ref.at[y * nx + x], bsem.at[2]).wait()
    wait(back_ref.at[pl.ds(0, nxy - 1)], bsem.at[1])
    back_wide[...] = back_ref[...].reshape(nxy * rows, piece).astype(F32)
    slots = experts * cap
    slot_ids = lax.broadcasted_iota(jnp.int32, (tok, slots), 1).astype(F32)

    def combine(i):
        zz = lax.rem(z + far_first(i), nz)
        mine = back_wide[pl.ds(zz, slots, stride=nz), :].astype(BF16)
        cols = columns[zz]
        total = jnp.zeros((tok, piece), F32)
        for s in range(top):
            chosen = jnp.where(slot_ids == cols[:, s : s + 1], 1.0, 0.0).astype(BF16)
            total = total + cols[:, top + s : top + s + 1] * jnp.dot(chosen, mine, preferred_element_type=F32)
        mixed[zz] = total.astype(BF16)

    def home_send(i):
        zz = lax.rem(z + far_first(i), nz)
        remote(mixed.at[zz], home.at[z], hsem.at[0], hsem.at[1], pos.dev(x, y, zz, c)).start()

    combine(0)

    def home_body(i, carry):
        combine(i)
        home_send(i - 1)
        return carry

    lax.fori_loop(1, nz, home_body, 0)
    own_home = pltpu.make_async_copy(mixed.at[z], home.at[z], hsem.at[2])
    own_home.start()

    for m in range(3):
        for w in range(parts):
            wait(weights[m].at[pl.ds(0, nxy - 1), :, pl.ds(w * lane, lane)], wsend.at[m, w])
            wait(wbuf.at[w, m, :, 0], fsend.at[m, w])
    for w in range(parts):
        for d, h, n in chains:
            for i in range(n):
                wait(land.at[w, d, h, i], rsend.at[w, d, h, i])
                for p in range(len(cuts)):
                    wait(hid_cut(w, mine_at, h, p), asend.at[w, d, h, i, p])
    for i in (ny - 2, ny - 1):
        t_sent(i)
    wait(back_ref.at[pl.ds(0, nxy - 1)], bsem.at[0])
    own_home.wait()
    wait(mixed.at[pl.ds(0, nz - 1)], hsem.at[0])
    wait(home.at[pl.ds(0, nz - 1)], hsem.at[1])
    for zh in range(nzh):
        left = jnp.concatenate([home[zh * nzl + zl] for zl in range(nzl)], axis=1)
        got = jnp.dot(left, perm_back[...], preferred_element_type=F32).astype(BF16)
        for seg, b in enumerate(blocks_of(zh)):
            final_ref[:, b] = got[:, seg * block : (seg + 1) * block]


def relay(pos, cid, token_count, tokens, names, probs, w_gate, w_up, w_down, cap):
    nx, ny, nz = pos.nx, pos.ny, pos.nz
    nxy = nx * ny
    _, depth, width = w_gate.shape
    tok, feats = tokens.shape
    piece = feats // nz
    lane = 128
    parts = width // lane
    rows = nz * cap
    wide = nx * lane
    dims = {
        "parts": parts, "rows": rows, "piece": piece, "top": 2, "depth": depth, "lane": lane, "tok": tok, "cap": cap
    }
    any_spec = pl.BlockSpec(memory_space=pl.ANY)
    vmem = pl.BlockSpec(memory_space=pltpu.VMEM)
    smem = pl.BlockSpec(memory_space=pltpu.SMEM)
    dma = pltpu.SemaphoreType.DMA
    return pl.pallas_call(
        lambda *refs: relay_kernel(pos, dims, refs),
        out_shape=jax.ShapeDtypeStruct((tok, feats), BF16),
        in_specs=[smem, vmem, vmem, vmem, any_spec, any_spec, any_spec],
        out_specs=vmem,
        scratch_shapes=[
            pltpu.VMEM((nz, tok, piece), BF16),
            pltpu.VMEM((8, tok), F32),
            pltpu.VMEM((feats // 2, feats // 2), BF16),
            pltpu.VMEM((nz, tok, 8), F32),
            pltpu.VMEM((nz, 8, tok), F32),
            pltpu.VMEM((nxy, rows, piece), BF16),
            pltpu.VMEM((nxy * rows, piece), F32),
            pltpu.VMEM((nz, tok, piece), BF16),
            pltpu.VMEM((nz, tok, piece), BF16),
            pltpu.VMEM((nz, tok, piece), BF16),
            pltpu.VMEM((nxy, rows, piece), BF16),
            pltpu.VMEM((ny, rows, nx * piece), BF16),
            pltpu.VMEM((parts, 3, ny, 2, depth, wide), BF16),
            pltpu.VMEM((parts, nz, rows, 2 * wide), BF16),
            pltpu.VMEM((parts, 2, 2, nz // 2, rows, wide), BF16),
            pltpu.VMEM((parts, nz, rows, wide), BF16),
            pltpu.VMEM((feats // 2, feats // 2), BF16),
            pltpu.VMEM((nz, rows, nx * piece), BF16),
            dma((2,)),
            dma((2,)),
            dma((12,)),
            dma((3, parts)),
            dma((3, parts)),
            dma((3, parts)),
            dma((3, parts)),
            dma((ny,)),
            dma((ny,)),
            dma((parts, 2, 2, nz // 2)),
            dma((parts, 2, 2, nz // 2)),
            dma((parts, 2, 2, nz // 2, 2)),
            dma((parts, 2, 2, nz // 2, 2)),
            dma((3,)),
            dma((3,)),
        ],
        compiler_params=pltpu.CompilerParams(
            collective_id=cid, has_side_effects=True, vmem_limit_bytes=56 * 1024 * 1024
        ),
        name="relay",
    )(token_count, tokens, names, probs, w_gate, w_up, w_down)


def shards(pos, tokens, routes, gate_prob, token_count, gate_weight, up_weight, down_weight):
    experts = gate_weight.shape[0]
    tok, top = routes.shape
    cap = min(tok, tok * top * 5 // (4 * experts))
    return relay(pos, 1, token_count, tokens, routes.T, gate_prob.T, gate_weight, up_weight, down_weight, cap)


def solution(mesh):
    nzl = mesh.shape["dp"]
    nx = mesh.shape["tensor"]
    nzh = 2
    ny = mesh.shape["expert"] // (2 * nzh)
    pos = Place(nx, ny, nzh * nzl, nzl)
    in_specs = (
        P(("expert", "dp"), "tensor"),
        P(("expert", "dp"), None),
        P(("expert", "dp"), None),
        P(("expert", "dp")),
        P(None, ("expert", "dp"), "tensor"),
        P(None, ("expert", "dp"), "tensor"),
        P(None, ("expert", "dp"), "tensor"),
    )
    out_specs = P(("expert", "dp"), "tensor")
    return jax.shard_map(
        functools.partial(shards, pos), mesh=mesh, in_specs=in_specs, out_specs=out_specs, check_vma=False
    )
```

```python
import functools

import jax
import jax.numpy as jnp
from jax import lax
from jax.experimental import pallas as pl
from jax.experimental.pallas import tpu as pltpu
from jax.sharding import PartitionSpec as P

MESH = pl.DeviceIdType.MESH
BF16 = jnp.bfloat16
F32 = jnp.float32


class Place:
    def __init__(self, nx, ny, nz, nzl):
        self.nx, self.ny, self.nz, self.nzl = nx, ny, nz, nzl
        self.nzh = nz // nzl

    def here(self):
        e = lax.axis_index("expert")
        x = lax.axis_index("tensor")
        zl = lax.axis_index("dp")
        core = lax.rem(e, 2)
        zh = lax.rem(e // 2, self.nzh)
        y = e // (2 * self.nzh)
        return x, y, zh * self.nzl + zl, core

    def dev(self, x, y, z, core):
        zh = z // self.nzl
        zl = lax.rem(z, self.nzl)
        return ((y * self.nzh + zh) * 2 + core, x, zl)


def signal_all(pos, x, y, z, c, barrier, xy, zring, core):
    n = 0
    if core:
        pl.semaphore_signal(barrier, inc=1, device_id=pos.dev(x, y, z, 1 - c), device_id_type=MESH)
        n += 1
    if zring == "ring":
        for dz in (1, pos.nz - 1):
            zz = lax.rem(z + dz, pos.nz)
            pl.semaphore_signal(barrier, inc=1, device_id=pos.dev(x, y, zz, c), device_id_type=MESH)
        n += 2
    if zring == "all":

        def zbody(k, carry):
            zz = lax.rem(z + k, pos.nz)
            pl.semaphore_signal(barrier, inc=1, device_id=pos.dev(x, y, zz, c), device_id_type=MESH)
            return carry

        lax.fori_loop(1, pos.nz, zbody, 0)
        n += pos.nz - 1
    if xy:

        def body(k, carry):
            xx = lax.rem(x + lax.rem(k, pos.nx), pos.nx)
            yy = lax.rem(y + k // pos.nx, pos.ny)
            pl.semaphore_signal(barrier, inc=1, device_id=pos.dev(xx, yy, z, c), device_id_type=MESH)
            return carry

        lax.fori_loop(1, pos.nx * pos.ny, body, 0)
        n += pos.nx * pos.ny - 1
    return n


def relay_kernel(pos, dims, refs):
    nx, ny, nz = pos.nx, pos.ny, pos.nz
    nxy = nx * ny
    parts, rows, piece, top = dims["parts"], dims["rows"], dims["piece"], dims["top"]
    depth, lane, tok, cap = dims["depth"], dims["lane"], dims["tok"], dims["cap"]
    feats = nz * piece
    half = nx * lane // 2
    (count_ref, tokens_ref, names_ref, prob_ref, wg_ref, wu_ref, wd_ref, final_ref) = refs[:8]
    (tok_ref, meta_ref, perm, columns, info_ref, back_ref, back_wide, mixed, home) = refs[8:17]
    (raw, out_tok, x_in, wbuf, part, land, hid, perm_back, out, result) = refs[17:27]
    (zsend, zrecv, loc, wsend, wrecv, fsend, frecv, tsend, trecv, rsend, rrecv, asend, arecv, bsem, hsem) = refs[27:]
    me = pos.here()
    x, y, z, c = me
    weights = (wg_ref, wu_ref, wd_ref)
    partner = pos.dev(x, y, z, 1 - c)

    def remote(src, dst, s, r, dev):
        return pltpu.make_async_remote_copy(src, dst, s, r, device_id=dev, device_id_type=MESH)

    def wait(ref, sem):
        pltpu.make_async_copy(ref, ref, sem).wait()

    barrier = pltpu.get_barrier_semaphore()
    partners = signal_all(pos, x, y, z, c, barrier, True, "all", True)

    nzl, nzh = pos.nzl, pos.nzh
    nseg = piece // depth
    block = nzl * depth
    lanes = lax.broadcasted_iota(jnp.int32, (1, nzl * piece), 1)
    inner = lax.rem(lanes, piece)
    source = (inner // depth) * block + (lanes // piece) * depth + lax.rem(inner, depth)
    ids = lax.broadcasted_iota(jnp.int32, (nseg * block, nzl * piece), 0)
    perm[...] = jnp.where(ids == source, 1.0, 0.0).astype(BF16)

    def blocks_of(zh):
        return [pl.ds((((seg // 2) * nzh + zh) * 2 + seg % 2) * block, block) for seg in range(nseg)]

    for zh in range(nzh):
        left = jnp.concatenate([tokens_ref[:, b] for b in blocks_of(zh)], axis=1)
        got = jnp.dot(left, perm[...], preferred_element_type=F32).astype(BF16)
        for zl in range(nzl):
            tok_ref[zh * nzl + zl] = got[:, zl * piece : (zl + 1) * piece]

    experts = nxy
    expert_ids = lax.broadcasted_iota(jnp.int32, (experts, tok), 0)
    live = lax.broadcasted_iota(jnp.int32, (experts, tok), 1) < count_ref[0]
    named = [(expert_ids == names_ref[s : s + 1, :]) & live for s in range(top)]
    either = jnp.where(functools.reduce(jnp.logical_or, named), 1.0, 0.0).astype(BF16)
    sooner = lax.broadcasted_iota(jnp.int32, (tok, tok), 0) < lax.broadcasted_iota(jnp.int32, (tok, tok), 1)
    rank = jnp.dot(either, jnp.where(sooner, 1.0, 0.0).astype(BF16), preferred_element_type=F32)
    meta_ref[...] = jnp.zeros_like(meta_ref)
    meta_ref[top : 2 * top, :] = prob_ref[...]
    for s in range(top):
        place = jnp.where(named[s], (expert_ids * cap).astype(F32) + rank + 1.0, 0.0)
        meta_ref[s : s + 1, :] = jnp.sum(place, axis=0, keepdims=True) - 1.0

    pl.semaphore_wait(barrier, partners)

    def far_first(i):
        return nz // 2 + (1 - 2 * lax.rem(i, 2)) * ((i + 1) // 2)

    def raw_send(i, carry):
        zz = lax.rem(z + far_first(i), nz)
        dev = pos.dev(x, y, zz, c)
        remote(tok_ref.at[zz], raw.at[z], zsend.at[0], zrecv.at[0], dev).start()
        remote(meta_ref, info_ref.at[z], zsend.at[1], zrecv.at[1], dev).start()
        return carry

    lax.fori_loop(0, nz - 1, raw_send, 0)
    own_raw = pltpu.make_async_copy(tok_ref.at[z], raw.at[z], loc.at[0])
    own_meta = pltpu.make_async_copy(meta_ref, info_ref.at[z], loc.at[1])
    own_raw.start()
    own_meta.start()

    def w_src(m, w, e):
        return weights[m].at[e, :, pl.ds(w * lane, lane)]

    def w_dst(m, w, xs, ys, cs):
        return wbuf.at[w, m, ys, cs, :, pl.ds(pl.multiple_of(xs * lane, lane), lane)]

    def w_start(w, mats):
        def body(k, carry):
            xx = lax.rem(x + lax.rem(k, nx), nx)
            yy = lax.rem(y + k // nx, ny)
            dev = pos.dev(xx, yy, z, c)
            for m in mats:
                remote(w_src(m, w, yy * nx + xx), w_dst(m, w, x, y, c), wsend.at[m], wrecv.at[m, w], dev).start()
            return carry

        lax.fori_loop(1, nxy, body, 0)
        for m in mats:
            pltpu.make_async_copy(w_src(m, w, y * nx + x), w_dst(m, w, x, y, c), loc.at[2 + 3 * w + m]).start()

    def w_forward(w, mats):
        for m in mats:
            pltpu.make_async_copy(w_src(m, w, y * nx + x), w_dst(m, w, x, y, c), loc.at[2 + 3 * w + m]).wait()
            wait(weights[m].at[pl.ds(0, nxy - 1), :, pl.ds(w * lane, lane)], wrecv.at[m, w])
            block = wbuf.at[w, m, :, c]
            remote(block, block, fsend, frecv.at[m, w], partner).start()

    def w_ready(w, mats):
        for m in mats:
            wait(wbuf.at[w, m, :, 0], frecv.at[m, w])

    w_start(0, (0, 1))

    own_raw.wait()
    own_meta.wait()
    for i, ref in ((1, info_ref), (0, raw)):
        wait(ref.at[pl.ds(0, nz - 1)], zsend.at[i])
        wait(ref.at[pl.ds(0, nz - 1)], zrecv.at[i])
    count = nx * rows

    def dy_of(i):
        return lax.rem(3 * nz - z - far_first(i), nz)

    def dispatch(i):
        yy = lax.rem(y + dy_of(i), ny)
        ids = lax.broadcasted_iota(jnp.int32, (count, raw.shape[1]), 0).astype(F32)
        base = (yy * count).astype(F32)
        picks = []
        for zz in range(nz):
            hit = None
            for s in range(top):
                same = ids == (info_ref[zz, s : s + 1, :] * nz + (zz - base))
                hit = same if hit is None else hit | same
            picks.append(jnp.where(hit, 1.0, 0.0).astype(BF16))
        pick = jnp.concatenate(picks, axis=1)
        got = jnp.dot(pick, raw[...].reshape(nz * tok, piece), preferred_element_type=F32).astype(BF16)
        out_tok[pl.ds(yy * nx, nx)] = got.reshape(nx, rows, piece)

    def t_dst(xs, ys):
        return x_in.at[ys, :, pl.ds(pl.multiple_of(xs * piece, piece), piece)]

    def t_send(i):
        dy = dy_of(i)
        yy = lax.rem(y + dy, ny)
        for dx in range(nx):
            xx = lax.rem(x + dx, nx)
            away = remote(out_tok.at[yy * nx + xx], t_dst(x, y), tsend.at[i], trecv.at[dy], pos.dev(xx, yy, z, c))
            if dx:
                away.start()
            else:

                @pl.when(dy != 0)
                def _():
                    away.start()

                @pl.when(dy == 0)
                def _():
                    pltpu.make_async_copy(out_tok.at[y * nx + x], t_dst(x, y), loc.at[11]).start()

    def t_sent(i):
        dy = dy_of(i)

        @pl.when(dy == 0)
        def _():
            wait(out_tok.at[pl.ds(0, nx - 1)], tsend.at[i])

        @pl.when(dy != 0)
        def _():
            wait(out_tok.at[pl.ds(0, nx)], tsend.at[i])

    dispatch(0)

    def d_body(i, carry):
        dispatch(i)
        t_send(i - 1)
        return carry

    lax.fori_loop(1, 5, d_body, 0)

    def d_late(i, carry):
        dispatch(i)
        t_sent(i - 5)
        t_send(i - 1)
        return carry

    lax.fori_loop(5, ny, d_late, 0)
    for zz in range(nz):
        columns[zz] = jnp.transpose(info_ref[zz])
    lanes = lax.broadcasted_iota(jnp.int32, (1, nseg * block), 1)
    inner = lax.rem(lanes, block)
    source = (inner // depth) * piece + (lanes // block) * depth + lax.rem(inner, depth)
    ids = lax.broadcasted_iota(jnp.int32, (nzl * piece, nseg * block), 0)
    perm_back[...] = jnp.where(ids == source, 1.0, 0.0).astype(BF16)
    t_sent(3)
    t_send(ny - 1)
    w_forward(0, (0, 1))
    t_sent(4)
    t_sent(5)
    w_start(1, (0, 1))

    def token_wait(i):
        dy = dy_of(i)

        @pl.when(dy == 0)
        def _():
            pltpu.make_async_copy(out_tok.at[y * nx + x], t_dst(x, y), loc.at[11]).wait()
            wait(x_in.at[0, :, pl.ds(0, (nx - 1) * piece)], trecv.at[0])

        @pl.when(dy != 0)
        def _():
            wait(x_in.at[0], trecv.at[dy])

    def spot(h, m):
        return slice((2 * h + m) * half, (2 * h + m + 1) * half)

    def first_part(order):
        js = [lax.rem(z + y + far_first(i), nz) for i in order]
        left = jnp.concatenate([x_in[j] for j in js], axis=0) if len(js) > 1 else x_in[js[0]]
        for m in range(2):
            res = jnp.dot(left, wbuf[0, m].reshape(ny * 2 * depth, nx * lane), preferred_element_type=F32).astype(BF16)
            for i, j in enumerate(js):
                for h in range(2):
                    part[0, j, :, spot(h, m)] = res[i * rows : (i + 1) * rows, h * half : (h + 1) * half]

    def product(w):
        wide = nx * lane
        for m in range(2):
            right = wbuf[w, m].reshape(ny * 2 * depth, wide)

            def body(i, carry):
                left = x_in[pl.ds(i * (ny // 2), ny // 2)].reshape(ny // 2 * rows, nx * piece)
                res = jnp.dot(left, right, preferred_element_type=F32).astype(BF16)
                span = pl.ds(i * (ny // 2), ny // 2)
                for h in range(2):
                    part[w, span, :, spot(h, m)] = res[:, h * half : (h + 1) * half].reshape(ny // 2, rows, half)
                return carry

            lax.fori_loop(0, 2, body, 0)

    step = (1, nz - 1)
    near = (pos.dev(x, y, lax.rem(z + 1, nz), c), pos.dev(x, y, lax.rem(z + nz - 1, nz), c))
    far = nz // 2
    chains = [(d, h, far if h == d else far - 1) for h in range(2) for d in range(2)]
    wide = nx * lane

    mine_at = lax.rem(z + y, nz)

    def at(d, k):
        return lax.rem(mine_at + (k if d == 0 else -k) + 2 * nz, nz)

    def rs_send(w, d, h, i, src):
        remote(src, land.at[w, d, h, i], rsend, rrecv.at[w, d, h, i], near[d]).start()

    def rs_start(w, hs=(0, 1)):
        for d, h, n in chains:
            if h in hs:
                rs_send(w, d, h, 0, part.at[w, at(d, n), :, pl.ds(h * wide, wide)])

    def rs_mid(w, i, hs=(0, 1)):
        ready = None
        for d, h, n in chains:
            if h in hs and i < n:
                slot = land.at[w, d, h, i - 1]
                wait(slot, rrecv.at[w, d, h, i - 1])
                mine = part[w, at(d, n - i), :, pl.ds(h * wide, wide)]
                slot[...] = (slot[...].astype(F32) + mine.astype(F32)).astype(BF16)
                if ready is not None:
                    rs_send(w, *ready)
                ready = (d, h, i, slot)
        if ready is not None:
            rs_send(w, *ready)

    def hid_half(w, j, h):
        return hid.at[w, j, :, pl.ds(h * half, half)]

    def ag_send(w, d, h, i, j):
        block = hid_half(w, j, h)
        remote(block, block, asend, arecv.at[w, d, h, i], near[d]).start()

    def rs_final(w, h):
        total = part[w, mine_at, :, pl.ds(h * wide, wide)].astype(F32)
        for d, hh, n in chains:
            if hh == h:
                slot = land.at[w, d, h, n - 1]
                wait(slot, rrecv.at[w, d, h, n - 1])
                total = total + slot[...].astype(F32)
        gate, up = total[:, :half], total[:, half:]
        hid[w, mine_at, :, h * half : (h + 1) * half] = (gate / (1.0 + jnp.exp(-gate)) * up).astype(BF16)

    def ag_start(w, h):
        for d, hh, n in chains:
            if hh == h:
                ag_send(w, d, h, 0, mine_at)

    def ag_mid(w, i, hs=(0, 1)):
        for d, h, n in chains:
            if h in hs and i <= n:
                j = at(d, -i)
                wait(hid_half(w, j, h), arecv.at[w, d, h, i - 1])
                if i < n:
                    ag_send(w, d, h, i, j)

    def o_src(xx, j):
        return out.at[j, :, pl.ds(pl.multiple_of(xx * piece, piece), piece)]

    def finish_rows(js):
        res = None
        for w in range(parts):
            left = jnp.concatenate([hid[w, j] for j in js], axis=0) if len(js) > 1 else hid[w, js[0]]
            right = wbuf[w, 2].reshape(ny * 2 * depth, wide)
            more = lax.dot_general(left, right, (((1,), (1,)), ((), ())), preferred_element_type=F32)
            res = more if res is None else res + more
        for i, j in enumerate(js):
            out[j] = res[i * rows : (i + 1) * rows].astype(BF16)

    def send_rows(js):
        for j in js:
            for dx in range(nx):
                xx = lax.rem(x + dx, nx)
                away = remote(o_src(xx, j), back_ref.at[y * nx + x], bsem.at[0], bsem.at[1], pos.dev(xx, j, z, c))
                if dx:
                    away.start()
                else:

                    @pl.when(j != y)
                    def _():
                        away.start()

                    @pl.when(j == y)
                    def _():
                        pltpu.make_async_copy(o_src(x, y), back_ref.at[y * nx + x], bsem.at[2]).start()

    w_ready(0, (0, 1))
    token_wait(0)
    token_wait(1)
    token_wait(2)
    first_part([0])
    first_part([1, 2])
    rs_start(0)
    token_wait(3)
    token_wait(4)
    first_part([3, 4])
    rs_mid(0, 1)
    token_wait(5)
    token_wait(6)
    first_part([5, 6])
    token_wait(7)
    first_part([7])
    w_start(2, (0,))
    rs_mid(0, 2)
    w_start(2, (1,))
    w_forward(1, (0, 1))
    rs_mid(0, 3)
    w_ready(1, (0, 1))
    product(1)
    rs_start(1)
    for h in range(2):
        rs_final(0, h)
        ag_start(0, h)
    rs_mid(1, 1)
    w_forward(2, (0, 1))
    w_ready(2, (0, 1))
    product(2)
    rs_start(2)
    rs_mid(1, 2)
    w_start(0, (2,))
    ag_mid(0, 1)
    rs_mid(2, 1)
    w_start(1, (2,))
    rs_mid(1, 3)
    w_start(2, (2,))
    rs_mid(2, 2)
    ag_mid(0, 2)
    rs_final(1, 0)
    rs_final(1, 1)
    rs_mid(2, 3)
    ag_start(1, 0)
    ag_start(1, 1)
    ag_mid(0, 3)
    w_forward(0, (2,))
    w_forward(1, (2,))
    for h in range(2):
        rs_final(2, h)
        ag_start(2, h)
    w_forward(2, (2,))
    ag_mid(0, 4)
    ag_mid(1, 1)
    for w in range(parts):
        w_ready(w, (2,))
    finish_rows([mine_at])
    send_rows([mine_at])
    ag_mid(2, 1)
    ag_mid(1, 2)
    finish_rows([at(0, 1), at(1, 1)])
    send_rows([at(0, 1), at(1, 1)])
    ag_mid(2, 2)
    ag_mid(1, 3)
    finish_rows([at(0, 2), at(1, 2)])
    send_rows([at(0, 2), at(1, 2)])
    ag_mid(2, 3)
    ag_mid(1, 4)
    finish_rows([at(0, 3), at(1, 3)])
    send_rows([at(0, 3), at(1, 3)])
    ag_mid(2, 4)
    finish_rows([at(0, 4)])
    send_rows([at(0, 4)])

    pltpu.make_async_copy(o_src(x, y), back_ref.at[y * nx + x], bsem.at[2]).wait()
    wait(back_ref.at[pl.ds(0, nxy - 1)], bsem.at[1])
    back_wide[...] = back_ref[...].reshape(nxy * rows, piece).astype(F32)
    slots = experts * cap
    slot_ids = lax.broadcasted_iota(jnp.int32, (tok, slots), 1).astype(F32)

    def combine(i):
        zz = lax.rem(z + far_first(i), nz)
        mine = back_wide[pl.ds(zz, slots, stride=nz), :].astype(BF16)
        cols = columns[zz]
        total = jnp.zeros((tok, piece), F32)
        for s in range(top):
            chosen = jnp.where(slot_ids == cols[:, s : s + 1], 1.0, 0.0).astype(BF16)
            total = total + cols[:, top + s : top + s + 1] * jnp.dot(chosen, mine, preferred_element_type=F32)
        mixed[zz] = total.astype(BF16)

    def home_send(i):
        zz = lax.rem(z + far_first(i), nz)
        remote(mixed.at[zz], home.at[z], hsem.at[0], hsem.at[1], pos.dev(x, y, zz, c)).start()

    combine(0)

    def home_body(i, carry):
        combine(i)
        home_send(i - 1)
        return carry

    lax.fori_loop(1, nz, home_body, 0)
    own_home = pltpu.make_async_copy(mixed.at[z], home.at[z], hsem.at[2])
    own_home.start()

    for m in range(3):
        wait(weights[m].at[pl.ds(0, nxy - 1)], wsend.at[m])
    wait(wbuf.at[:, :, :, 0], fsend)
    wait(part.at[:, pl.ds(0, nz - 1)], rsend)
    wait(hid.at[:, pl.ds(0, nz - 1)], asend)
    for i in (ny - 2, ny - 1):
        t_sent(i)
    wait(back_ref.at[pl.ds(0, nxy - 1)], bsem.at[0])
    own_home.wait()
    wait(mixed.at[pl.ds(0, nz - 1)], hsem.at[0])
    wait(home.at[pl.ds(0, nz - 1)], hsem.at[1])
    for zh in range(nzh):
        left = jnp.concatenate([home[zh * nzl + zl] for zl in range(nzl)], axis=1)
        got = jnp.dot(left, perm_back[...], preferred_element_type=F32).astype(BF16)
        for seg, b in enumerate(blocks_of(zh)):
            result[:, b] = got[:, seg * block : (seg + 1) * block]
    leave = pltpu.make_async_copy(result, final_ref, hsem.at[2])
    leave.start()
    leave.wait()


def relay(pos, cid, token_count, tokens, names, probs, w_gate, w_up, w_down, cap):
    nx, ny, nz = pos.nx, pos.ny, pos.nz
    nxy = nx * ny
    _, depth, width = w_gate.shape
    tok, feats = tokens.shape
    piece = feats // nz
    lane = 128
    parts = width // lane
    rows = nz * cap
    wide = nx * lane
    dims = {
        "parts": parts, "rows": rows, "piece": piece, "top": 2, "depth": depth, "lane": lane, "tok": tok, "cap": cap
    }
    any_spec = pl.BlockSpec(memory_space=pl.ANY)
    vmem = pl.BlockSpec(memory_space=pltpu.VMEM)
    smem = pl.BlockSpec(memory_space=pltpu.SMEM)
    dma = pltpu.SemaphoreType.DMA
    return pl.pallas_call(
        lambda *refs: relay_kernel(pos, dims, refs),
        out_shape=jax.ShapeDtypeStruct((tok, feats), BF16),
        in_specs=[smem, vmem, vmem, vmem, any_spec, any_spec, any_spec],
        out_specs=any_spec,
        scratch_shapes=[
            pltpu.VMEM((nz, tok, piece), BF16),
            pltpu.VMEM((8, tok), F32),
            pltpu.VMEM((feats // 2, feats // 2), BF16),
            pltpu.VMEM((nz, tok, 8), F32),
            pltpu.VMEM((nz, 8, tok), F32),
            pltpu.VMEM((nxy, rows, piece), BF16),
            pltpu.VMEM((nxy * rows, piece), F32),
            pltpu.VMEM((nz, tok, piece), BF16),
            pltpu.VMEM((nz, tok, piece), BF16),
            pltpu.VMEM((nz, tok, piece), BF16),
            pltpu.VMEM((nxy, rows, piece), BF16),
            pltpu.VMEM((ny, rows, nx * piece), BF16),
            pltpu.VMEM((parts, 3, ny, 2, depth, wide), BF16),
            pltpu.VMEM((parts, nz, rows, 2 * wide), BF16),
            pltpu.VMEM((parts, 2, 2, nz // 2, rows, wide), BF16),
            pltpu.VMEM((parts, nz, rows, wide), BF16),
            pltpu.VMEM((feats // 2, feats // 2), BF16),
            pltpu.VMEM((nz, rows, nx * piece), BF16),
            pltpu.VMEM((tok, feats), BF16),
            dma((2,)),
            dma((2,)),
            dma((12,)),
            dma((3,)),
            dma((3, parts)),
            dma,
            dma((3, parts)),
            dma((ny,)),
            dma((ny,)),
            dma,
            dma((parts, 2, 2, nz // 2)),
            dma,
            dma((parts, 2, 2, nz // 2)),
            dma((3,)),
            dma((3,)),
        ],
        compiler_params=pltpu.CompilerParams(
            collective_id=cid, has_side_effects=True, vmem_limit_bytes=56 * 1024 * 1024
        ),
        name="relay",
    )(token_count, tokens, names, probs, w_gate, w_up, w_down)


def shards(pos, tokens, routes, gate_prob, token_count, gate_weight, up_weight, down_weight):
    experts = gate_weight.shape[0]
    tok, top = routes.shape
    cap = min(tok, tok * top * 5 // (4 * experts))
    return relay(pos, 1, token_count, tokens, routes.T, gate_prob.T, gate_weight, up_weight, down_weight, cap)


def solution(mesh):
    nzl = mesh.shape["dp"]
    nx = mesh.shape["tensor"]
    nzh = 2
    ny = mesh.shape["expert"] // (2 * nzh)
    pos = Place(nx, ny, nzh * nzl, nzl)
    in_specs = (
        P(("expert", "dp"), "tensor"),
        P(("expert", "dp"), None),
        P(("expert", "dp"), None),
        P(("expert", "dp")),
        P(None, ("expert", "dp"), "tensor"),
        P(None, ("expert", "dp"), "tensor"),
        P(None, ("expert", "dp"), "tensor"),
    )
    out_specs = P(("expert", "dp"), "tensor")
    return jax.shard_map(
        functools.partial(shards, pos), mesh=mesh, in_specs=in_specs, out_specs=out_specs, check_vma=False
    )
```

```python
import functools

import jax
import jax.numpy as jnp
from jax import lax
from jax.experimental import pallas as pl
from jax.experimental.pallas import tpu as pltpu
from jax.sharding import PartitionSpec as P

MESH = pl.DeviceIdType.MESH
BF16 = jnp.bfloat16
F32 = jnp.float32


class Place:
    def __init__(self, nx, ny, nz, nzl):
        self.nx, self.ny, self.nz, self.nzl = nx, ny, nz, nzl
        self.nzh = nz // nzl

    def here(self):
        e = lax.axis_index("expert")
        x = lax.axis_index("tensor")
        zl = lax.axis_index("dp")
        core = lax.rem(e, 2)
        zh = lax.rem(e // 2, self.nzh)
        y = e // (2 * self.nzh)
        return x, y, zh * self.nzl + zl, core

    def dev(self, x, y, z, core):
        zh = z // self.nzl
        zl = lax.rem(z, self.nzl)
        return ((y * self.nzh + zh) * 2 + core, x, zl)


def signal_all(pos, x, y, z, c, barrier, xy, zring, core):
    n = 0
    if core:
        pl.semaphore_signal(barrier, inc=1, device_id=pos.dev(x, y, z, 1 - c), device_id_type=MESH)
        n += 1
    if zring == "ring":
        for dz in (1, pos.nz - 1):
            zz = lax.rem(z + dz, pos.nz)
            pl.semaphore_signal(barrier, inc=1, device_id=pos.dev(x, y, zz, c), device_id_type=MESH)
        n += 2
    if zring == "all":

        def zbody(k, carry):
            zz = lax.rem(z + k, pos.nz)
            pl.semaphore_signal(barrier, inc=1, device_id=pos.dev(x, y, zz, c), device_id_type=MESH)
            return carry

        lax.fori_loop(1, pos.nz, zbody, 0)
        n += pos.nz - 1
    if xy:

        def body(k, carry):
            xx = lax.rem(x + lax.rem(k, pos.nx), pos.nx)
            yy = lax.rem(y + k // pos.nx, pos.ny)
            pl.semaphore_signal(barrier, inc=1, device_id=pos.dev(xx, yy, z, c), device_id_type=MESH)
            return carry

        lax.fori_loop(1, pos.nx * pos.ny, body, 0)
        n += pos.nx * pos.ny - 1
    return n


def relay_kernel(pos, dims, refs):
    nx, ny, nz = pos.nx, pos.ny, pos.nz
    nxy = nx * ny
    parts, rows, piece, top = dims["parts"], dims["rows"], dims["piece"], dims["top"]
    depth, lane, tok, cap = dims["depth"], dims["lane"], dims["tok"], dims["cap"]
    feats = nz * piece
    half = nx * lane // 2
    (count_ref, tokens_ref, names_ref, prob_ref, wg_ref, wu_ref, wd_ref, final_ref) = refs[:8]
    (tok_ref, meta_ref, perm, columns, info_ref, back_ref, back_wide, mixed, home) = refs[8:17]
    (raw, out_tok, x_in, wbuf, part, land, hid, perm_back, out, result) = refs[17:27]
    (zsend, zrecv, loc, wsend, wrecv, fsend, frecv, tsend, trecv, rsend, rrecv, asend, arecv, bsem, hsem) = refs[27:]
    me = pos.here()
    x, y, z, c = me
    weights = (wg_ref, wu_ref, wd_ref)
    partner = pos.dev(x, y, z, 1 - c)

    def remote(src, dst, s, r, dev):
        return pltpu.make_async_remote_copy(src, dst, s, r, device_id=dev, device_id_type=MESH)

    def wait(ref, sem):
        pltpu.make_async_copy(ref, ref, sem).wait()

    barrier = pltpu.get_barrier_semaphore()
    partners = signal_all(pos, x, y, z, c, barrier, True, "all", True)

    nzl, nzh = pos.nzl, pos.nzh
    nseg = piece // depth
    block = nzl * depth
    lanes = lax.broadcasted_iota(jnp.int32, (1, nzl * piece), 1)
    inner = lax.rem(lanes, piece)
    source = (inner // depth) * block + (lanes // piece) * depth + lax.rem(inner, depth)
    ids = lax.broadcasted_iota(jnp.int32, (nseg * block, nzl * piece), 0)
    perm[...] = jnp.where(ids == source, 1.0, 0.0).astype(BF16)

    def blocks_of(zh):
        return [pl.ds((((seg // 2) * nzh + zh) * 2 + seg % 2) * block, block) for seg in range(nseg)]

    for zh in range(nzh):
        left = jnp.concatenate([tokens_ref[:, b] for b in blocks_of(zh)], axis=1)
        got = jnp.dot(left, perm[...], preferred_element_type=F32).astype(BF16)
        for zl in range(nzl):
            tok_ref[zh * nzl + zl] = got[:, zl * piece : (zl + 1) * piece]

    experts = nxy
    expert_ids = lax.broadcasted_iota(jnp.int32, (experts, tok), 0)
    live = lax.broadcasted_iota(jnp.int32, (experts, tok), 1) < count_ref[0]
    named = [(expert_ids == names_ref[s : s + 1, :]) & live for s in range(top)]
    either = jnp.where(functools.reduce(jnp.logical_or, named), 1.0, 0.0).astype(BF16)
    sooner = lax.broadcasted_iota(jnp.int32, (tok, tok), 0) < lax.broadcasted_iota(jnp.int32, (tok, tok), 1)
    rank = jnp.dot(either, jnp.where(sooner, 1.0, 0.0).astype(BF16), preferred_element_type=F32)
    meta_ref[...] = jnp.zeros_like(meta_ref)
    meta_ref[top : 2 * top, :] = prob_ref[...]
    for s in range(top):
        place = jnp.where(named[s], (expert_ids * cap).astype(F32) + rank + 1.0, 0.0)
        meta_ref[s : s + 1, :] = jnp.sum(place, axis=0, keepdims=True) - 1.0

    pl.semaphore_wait(barrier, partners)

    def far_first(i):
        return nz // 2 + (1 - 2 * lax.rem(i, 2)) * ((i + 1) // 2)

    def raw_send(i, carry):
        zz = lax.rem(z + far_first(i), nz)
        dev = pos.dev(x, y, zz, c)
        remote(tok_ref.at[zz], raw.at[z], zsend.at[0], zrecv.at[0], dev).start()
        remote(meta_ref, info_ref.at[z], zsend.at[1], zrecv.at[1], dev).start()
        return carry

    lax.fori_loop(0, nz - 1, raw_send, 0)
    own_raw = pltpu.make_async_copy(tok_ref.at[z], raw.at[z], loc.at[0])
    own_meta = pltpu.make_async_copy(meta_ref, info_ref.at[z], loc.at[1])
    own_raw.start()
    own_meta.start()

    def w_src(m, w, e):
        return weights[m].at[e, :, pl.ds(w * lane, lane)]

    def w_dst(m, w, xs, ys, cs):
        return wbuf.at[w, m, ys, cs, :, pl.ds(pl.multiple_of(xs * lane, lane), lane)]

    def w_start(w, mats):
        def body(k, carry):
            xx = lax.rem(x + lax.rem(k, nx) + 1, nx)
            yy = lax.rem(y + far_first(k // nx), ny)
            dev = pos.dev(xx, yy, z, c)
            for m in mats:
                remote(w_src(m, w, yy * nx + xx), w_dst(m, w, x, y, c), wsend.at[m], wrecv.at[m, w], dev).start()
            return carry

        lax.fori_loop(0, nxy - 1, body, 0)
        for m in mats:
            pltpu.make_async_copy(w_src(m, w, y * nx + x), w_dst(m, w, x, y, c), loc.at[2 + 3 * w + m]).start()

    def w_forward(w, mats):
        for m in mats:
            pltpu.make_async_copy(w_src(m, w, y * nx + x), w_dst(m, w, x, y, c), loc.at[2 + 3 * w + m]).wait()
            wait(weights[m].at[pl.ds(0, nxy - 1), :, pl.ds(w * lane, lane)], wrecv.at[m, w])
            block = wbuf.at[w, m, :, c]
            remote(block, block, fsend, frecv.at[m, w], partner).start()

    def w_ready(w, mats):
        for m in mats:
            wait(wbuf.at[w, m, :, 0], frecv.at[m, w])

    w_start(0, (0, 1))

    own_raw.wait()
    own_meta.wait()
    for i, ref in ((1, info_ref), (0, raw)):
        wait(ref.at[pl.ds(0, nz - 1)], zsend.at[i])
        wait(ref.at[pl.ds(0, nz - 1)], zrecv.at[i])
    count = nx * rows

    def dy_of(i):
        return lax.rem(6 * nz - 3 * (z + far_first(i)), nz)

    def dispatch(i):
        yy = lax.rem(y + dy_of(i), ny)
        ids = lax.broadcasted_iota(jnp.int32, (count, raw.shape[1]), 0).astype(F32)
        base = (yy * count).astype(F32)
        picks = []
        for zz in range(nz):
            hit = None
            for s in range(top):
                same = ids == (info_ref[zz, s : s + 1, :] * nz + (zz - base))
                hit = same if hit is None else hit | same
            picks.append(jnp.where(hit, 1.0, 0.0).astype(BF16))
        pick = jnp.concatenate(picks, axis=1)
        got = jnp.dot(pick, raw[...].reshape(nz * tok, piece), preferred_element_type=F32).astype(BF16)
        out_tok[pl.ds(yy * nx, nx)] = got.reshape(nx, rows, piece)

    def t_dst(xs, ys):
        return x_in.at[ys, :, pl.ds(pl.multiple_of(xs * piece, piece), piece)]

    def t_send(i):
        dy = dy_of(i)
        yy = lax.rem(y + dy, ny)
        for dx in range(nx):
            xx = lax.rem(x + dx, nx)
            away = remote(out_tok.at[yy * nx + xx], t_dst(x, y), tsend.at[i], trecv.at[dy], pos.dev(xx, yy, z, c))
            if dx:
                away.start()
            else:

                @pl.when(dy != 0)
                def _():
                    away.start()

                @pl.when(dy == 0)
                def _():
                    pltpu.make_async_copy(out_tok.at[y * nx + x], t_dst(x, y), loc.at[11]).start()

    def t_sent(i):
        dy = dy_of(i)

        @pl.when(dy == 0)
        def _():
            wait(out_tok.at[pl.ds(0, nx - 1)], tsend.at[i])

        @pl.when(dy != 0)
        def _():
            wait(out_tok.at[pl.ds(0, nx)], tsend.at[i])

    dispatch(0)

    def d_body(i, carry):
        dispatch(i)
        t_send(i - 1)
        return carry

    lax.fori_loop(1, 5, d_body, 0)

    def d_late(i, carry):
        dispatch(i)
        t_sent(i - 5)
        t_send(i - 1)
        return carry

    lax.fori_loop(5, ny, d_late, 0)
    for zz in range(nz):
        columns[zz] = jnp.transpose(info_ref[zz])
    lanes = lax.broadcasted_iota(jnp.int32, (1, nseg * block), 1)
    inner = lax.rem(lanes, block)
    source = (inner // depth) * piece + (lanes // block) * depth + lax.rem(inner, depth)
    ids = lax.broadcasted_iota(jnp.int32, (nzl * piece, nseg * block), 0)
    perm_back[...] = jnp.where(ids == source, 1.0, 0.0).astype(BF16)
    t_sent(3)
    t_send(ny - 1)
    w_forward(0, (0, 1))
    t_sent(4)
    t_sent(5)
    w_start(1, (0, 1))

    def token_wait(i):
        dy = dy_of(i)

        @pl.when(dy == 0)
        def _():
            pltpu.make_async_copy(out_tok.at[y * nx + x], t_dst(x, y), loc.at[11]).wait()
            wait(x_in.at[0, :, pl.ds(0, (nx - 1) * piece)], trecv.at[0])

        @pl.when(dy != 0)
        def _():
            wait(x_in.at[0], trecv.at[dy])

    def spot(h, m):
        return slice((2 * h + m) * half, (2 * h + m + 1) * half)

    def first_part(order):
        js = [lax.rem(3 * (z + far_first(i)) + y, nz) for i in order]
        left = jnp.concatenate([x_in[j] for j in js], axis=0) if len(js) > 1 else x_in[js[0]]
        for m in range(2):
            res = jnp.dot(left, wbuf[0, m].reshape(ny * 2 * depth, nx * lane), preferred_element_type=F32).astype(BF16)
            for i, j in enumerate(js):
                for h in range(2):
                    part[0, j, :, spot(h, m)] = res[i * rows : (i + 1) * rows, h * half : (h + 1) * half]

    def product(w):
        wide = nx * lane
        for m in range(2):
            right = wbuf[w, m].reshape(ny * 2 * depth, wide)

            def body(i, carry):
                left = x_in[pl.ds(i * (ny // 2), ny // 2)].reshape(ny // 2 * rows, nx * piece)
                res = jnp.dot(left, right, preferred_element_type=F32).astype(BF16)
                span = pl.ds(i * (ny // 2), ny // 2)
                for h in range(2):
                    part[w, span, :, spot(h, m)] = res[:, h * half : (h + 1) * half].reshape(ny // 2, rows, half)
                return carry

            lax.fori_loop(0, 2, body, 0)

    step = (1, nz - 1)
    near = (pos.dev(x, y, lax.rem(z + 1, nz), c), pos.dev(x, y, lax.rem(z + nz - 1, nz), c))
    far = nz // 2
    chains = [(d, h, far if h == d else far - 1) for h in range(2) for d in range(2)]
    wide = nx * lane

    mine_at = lax.rem(3 * z + y, nz)

    def at(d, k):
        return lax.rem(3 * (z + (k if d == 0 else -k)) + y + 2 * nz, nz)

    def rs_send(w, d, h, i, src):
        remote(src, land.at[w, d, h, i], rsend, rrecv.at[w, d, h, i], near[d]).start()

    def rs_start(w, hs=(0, 1)):
        for d, h, n in chains:
            if h in hs:
                rs_send(w, d, h, 0, part.at[w, at(d, n), :, pl.ds(h * wide, wide)])

    def rs_mid(w, i, hs=(0, 1)):
        ready = None
        for d, h, n in chains:
            if h in hs and i < n:
                slot = land.at[w, d, h, i - 1]
                wait(slot, rrecv.at[w, d, h, i - 1])
                mine = part[w, at(d, n - i), :, pl.ds(h * wide, wide)]
                slot[...] = (slot[...].astype(F32) + mine.astype(F32)).astype(BF16)
                if ready is not None:
                    rs_send(w, *ready)
                ready = (d, h, i, slot)
        if ready is not None:
            rs_send(w, *ready)

    def hid_half(w, j, h):
        return hid.at[w, j, :, pl.ds(h * half, half)]

    def ag_send(w, d, h, i, j):
        block = hid_half(w, j, h)
        remote(block, block, asend, arecv.at[w, d, h, i], near[d]).start()

    def rs_final(w, h):
        total = part[w, mine_at, :, pl.ds(h * wide, wide)].astype(F32)
        for d, hh, n in chains:
            if hh == h:
                slot = land.at[w, d, h, n - 1]
                wait(slot, rrecv.at[w, d, h, n - 1])
                total = total + slot[...].astype(F32)
        gate, up = total[:, :half], total[:, half:]
        hid[w, mine_at, :, h * half : (h + 1) * half] = (gate / (1.0 + jnp.exp(-gate)) * up).astype(BF16)

    def ag_start(w, h):
        for d, hh, n in chains:
            if hh == h:
                ag_send(w, d, h, 0, mine_at)

    def ag_mid(w, i, hs=(0, 1)):
        for d, h, n in chains:
            if h in hs and i <= n:
                j = at(d, -i)
                wait(hid_half(w, j, h), arecv.at[w, d, h, i - 1])
                if i < n:
                    ag_send(w, d, h, i, j)

    def o_src(xx, j):
        return out.at[j, :, pl.ds(pl.multiple_of(xx * piece, piece), piece)]

    def finish_rows(js):
        res = None
        for w in range(parts):
            left = jnp.concatenate([hid[w, j] for j in js], axis=0) if len(js) > 1 else hid[w, js[0]]
            right = wbuf[w, 2].reshape(ny * 2 * depth, wide)
            more = lax.dot_general(left, right, (((1,), (1,)), ((), ())), preferred_element_type=F32)
            res = more if res is None else res + more
        for i, j in enumerate(js):
            out[j] = res[i * rows : (i + 1) * rows].astype(BF16)

    def send_rows(js):
        for j in js:
            for dx in range(nx):
                xx = lax.rem(x + dx, nx)
                away = remote(o_src(xx, j), back_ref.at[y * nx + x], bsem.at[0], bsem.at[1], pos.dev(xx, j, z, c))
                if dx:
                    away.start()
                else:

                    @pl.when(j != y)
                    def _():
                        away.start()

                    @pl.when(j == y)
                    def _():
                        pltpu.make_async_copy(o_src(x, y), back_ref.at[y * nx + x], bsem.at[2]).start()

    w_ready(0, (0, 1))
    token_wait(0)
    token_wait(1)
    token_wait(2)
    first_part([0])
    first_part([1, 2])
    rs_start(0)
    token_wait(3)
    token_wait(4)
    first_part([3, 4])
    rs_mid(0, 1)
    token_wait(5)
    token_wait(6)
    first_part([5, 6])
    token_wait(7)
    first_part([7])
    w_start(2, (0,))
    rs_mid(0, 2)
    w_start(2, (1,))
    w_forward(1, (0, 1))
    rs_mid(0, 3)
    w_ready(1, (0, 1))
    product(1)
    rs_start(1)
    for h in range(2):
        rs_final(0, h)
        ag_start(0, h)
    rs_mid(1, 1)
    w_forward(2, (0, 1))
    w_ready(2, (0, 1))
    product(2)
    rs_start(2)
    rs_mid(1, 2)
    w_start(0, (2,))
    ag_mid(0, 1)
    rs_mid(2, 1)
    w_start(1, (2,))
    rs_mid(1, 3)
    w_start(2, (2,))
    rs_mid(2, 2)
    ag_mid(0, 2)
    rs_final(1, 0)
    rs_final(1, 1)
    rs_mid(2, 3)
    ag_start(1, 0)
    ag_start(1, 1)
    ag_mid(0, 3)
    w_forward(0, (2,))
    w_forward(1, (2,))
    for h in range(2):
        rs_final(2, h)
        ag_start(2, h)
    w_forward(2, (2,))
    ag_mid(0, 4)
    ag_mid(1, 1)
    for w in range(parts):
        w_ready(w, (2,))
    finish_rows([mine_at])
    send_rows([mine_at])
    ag_mid(2, 1)
    ag_mid(1, 2)
    finish_rows([at(0, 1), at(1, 1)])
    send_rows([at(0, 1), at(1, 1)])
    ag_mid(2, 2)
    ag_mid(1, 3)
    finish_rows([at(0, 2), at(1, 2)])
    send_rows([at(0, 2), at(1, 2)])
    ag_mid(2, 3)
    ag_mid(1, 4)
    finish_rows([at(0, 3), at(1, 3)])
    send_rows([at(0, 3), at(1, 3)])
    ag_mid(2, 4)
    finish_rows([at(0, 4)])
    send_rows([at(0, 4)])

    pltpu.make_async_copy(o_src(x, y), back_ref.at[y * nx + x], bsem.at[2]).wait()
    wait(back_ref.at[pl.ds(0, nxy - 1)], bsem.at[1])
    back_wide[...] = back_ref[...].reshape(nxy * rows, piece).astype(F32)
    slots = experts * cap
    slot_ids = lax.broadcasted_iota(jnp.int32, (tok, slots), 1).astype(F32)

    def combine(i):
        zz = lax.rem(z + far_first(i), nz)
        mine = back_wide[pl.ds(zz, slots, stride=nz), :].astype(BF16)
        cols = columns[zz]
        total = jnp.zeros((tok, piece), F32)
        for s in range(top):
            chosen = jnp.where(slot_ids == cols[:, s : s + 1], 1.0, 0.0).astype(BF16)
            total = total + cols[:, top + s : top + s + 1] * jnp.dot(chosen, mine, preferred_element_type=F32)
        mixed[zz] = total.astype(BF16)

    def home_send(i):
        zz = lax.rem(z + far_first(i), nz)
        remote(mixed.at[zz], home.at[z], hsem.at[0], hsem.at[1], pos.dev(x, y, zz, c)).start()

    combine(0)

    def home_body(i, carry):
        combine(i)
        home_send(i - 1)
        return carry

    lax.fori_loop(1, nz, home_body, 0)
    own_home = pltpu.make_async_copy(mixed.at[z], home.at[z], hsem.at[2])
    own_home.start()

    for m in range(3):
        wait(weights[m].at[pl.ds(0, nxy - 1)], wsend.at[m])
    wait(wbuf.at[:, :, :, 0], fsend)
    wait(part.at[:, pl.ds(0, nz - 1)], rsend)
    wait(hid.at[:, pl.ds(0, nz - 1)], asend)
    for i in (ny - 2, ny - 1):
        t_sent(i)
    wait(back_ref.at[pl.ds(0, nxy - 1)], bsem.at[0])
    own_home.wait()
    wait(mixed.at[pl.ds(0, nz - 1)], hsem.at[0])
    wait(home.at[pl.ds(0, nz - 1)], hsem.at[1])
    for zh in range(nzh):
        left = jnp.concatenate([home[zh * nzl + zl] for zl in range(nzl)], axis=1)
        got = jnp.dot(left, perm_back[...], preferred_element_type=F32).astype(BF16)
        for seg, b in enumerate(blocks_of(zh)):
            result[:, b] = got[:, seg * block : (seg + 1) * block]
    leave = pltpu.make_async_copy(result, final_ref, hsem.at[2])
    leave.start()
    leave.wait()


def relay(pos, cid, token_count, tokens, names, probs, w_gate, w_up, w_down, cap):
    nx, ny, nz = pos.nx, pos.ny, pos.nz
    nxy = nx * ny
    _, depth, width = w_gate.shape
    tok, feats = tokens.shape
    piece = feats // nz
    lane = 128
    parts = width // lane
    rows = nz * cap
    wide = nx * lane
    dims = {
        "parts": parts, "rows": rows, "piece": piece, "top": 2, "depth": depth, "lane": lane, "tok": tok, "cap": cap
    }
    any_spec = pl.BlockSpec(memory_space=pl.ANY)
    vmem = pl.BlockSpec(memory_space=pltpu.VMEM)
    smem = pl.BlockSpec(memory_space=pltpu.SMEM)
    dma = pltpu.SemaphoreType.DMA
    return pl.pallas_call(
        lambda *refs: relay_kernel(pos, dims, refs),
        out_shape=jax.ShapeDtypeStruct((tok, feats), BF16),
        in_specs=[smem, vmem, vmem, vmem, any_spec, any_spec, any_spec],
        out_specs=any_spec,
        scratch_shapes=[
            pltpu.VMEM((nz, tok, piece), BF16),
            pltpu.VMEM((8, tok), F32),
            pltpu.VMEM((feats // 2, feats // 2), BF16),
            pltpu.VMEM((nz, tok, 8), F32),
            pltpu.VMEM((nz, 8, tok), F32),
            pltpu.VMEM((nxy, rows, piece), BF16),
            pltpu.VMEM((nxy * rows, piece), F32),
            pltpu.VMEM((nz, tok, piece), BF16),
            pltpu.VMEM((nz, tok, piece), BF16),
            pltpu.VMEM((nz, tok, piece), BF16),
            pltpu.VMEM((nxy, rows, piece), BF16),
            pltpu.VMEM((ny, rows, nx * piece), BF16),
            pltpu.VMEM((parts, 3, ny, 2, depth, wide), BF16),
            pltpu.VMEM((parts, nz, rows, 2 * wide), BF16),
            pltpu.VMEM((parts, 2, 2, nz // 2, rows, wide), BF16),
            pltpu.VMEM((parts, nz, rows, wide), BF16),
            pltpu.VMEM((feats // 2, feats // 2), BF16),
            pltpu.VMEM((nz, rows, nx * piece), BF16),
            pltpu.VMEM((tok, feats), BF16),
            dma((2,)),
            dma((2,)),
            dma((12,)),
            dma((3,)),
            dma((3, parts)),
            dma,
            dma((3, parts)),
            dma((ny,)),
            dma((ny,)),
            dma,
            dma((parts, 2, 2, nz // 2)),
            dma,
            dma((parts, 2, 2, nz // 2)),
            dma((3,)),
            dma((3,)),
        ],
        compiler_params=pltpu.CompilerParams(
            collective_id=cid, has_side_effects=True, vmem_limit_bytes=56 * 1024 * 1024
        ),
        name="relay",
    )(token_count, tokens, names, probs, w_gate, w_up, w_down)


def shards(pos, tokens, routes, gate_prob, token_count, gate_weight, up_weight, down_weight):
    experts = gate_weight.shape[0]
    tok, top = routes.shape
    cap = min(tok, tok * top * 5 // (4 * experts))
    return relay(pos, 1, token_count, tokens, routes.T, gate_prob.T, gate_weight, up_weight, down_weight, cap)


def solution(mesh):
    nzl = mesh.shape["dp"]
    nx = mesh.shape["tensor"]
    nzh = 2
    ny = mesh.shape["expert"] // (2 * nzh)
    pos = Place(nx, ny, nzh * nzl, nzl)
    in_specs = (
        P(("expert", "dp"), "tensor"),
        P(("expert", "dp"), None),
        P(("expert", "dp"), None),
        P(("expert", "dp")),
        P(None, ("expert", "dp"), "tensor"),
        P(None, ("expert", "dp"), "tensor"),
        P(None, ("expert", "dp"), "tensor"),
    )
    out_specs = P(("expert", "dp"), "tensor")
    return jax.shard_map(
        functools.partial(shards, pos), mesh=mesh, in_specs=in_specs, out_specs=out_specs, check_vma=False
    )
```

```python
import functools

import jax
import jax.numpy as jnp
from jax import lax
from jax.experimental import pallas as pl
from jax.experimental.pallas import tpu as pltpu
from jax.sharding import PartitionSpec as P

MESH = pl.DeviceIdType.MESH
BF16 = jnp.bfloat16
F32 = jnp.float32


class Place:
    def __init__(self, nx, ny, nz, nzl):
        self.nx, self.ny, self.nz, self.nzl = nx, ny, nz, nzl
        self.nzh = nz // nzl

    def here(self):
        e = lax.axis_index("expert")
        x = lax.axis_index("tensor")
        zl = lax.axis_index("dp")
        core = lax.rem(e, 2)
        zh = lax.rem(e // 2, self.nzh)
        y = e // (2 * self.nzh)
        return x, y, zh * self.nzl + zl, core

    def dev(self, x, y, z, core):
        zh = z // self.nzl
        zl = lax.rem(z, self.nzl)
        return ((y * self.nzh + zh) * 2 + core, x, zl)


def signal_all(pos, x, y, z, c, barrier, xy, zring, core):
    n = 0
    if core:
        pl.semaphore_signal(barrier, inc=1, device_id=pos.dev(x, y, z, 1 - c), device_id_type=MESH)
        n += 1
    if zring == "ring":
        for dz in (1, pos.nz - 1):
            zz = lax.rem(z + dz, pos.nz)
            pl.semaphore_signal(barrier, inc=1, device_id=pos.dev(x, y, zz, c), device_id_type=MESH)
        n += 2
    if zring == "all":

        def zbody(k, carry):
            zz = lax.rem(z + k, pos.nz)
            pl.semaphore_signal(barrier, inc=1, device_id=pos.dev(x, y, zz, c), device_id_type=MESH)
            return carry

        lax.fori_loop(1, pos.nz, zbody, 0)
        n += pos.nz - 1
    if xy:

        def body(k, carry):
            xx = lax.rem(x + lax.rem(k, pos.nx), pos.nx)
            yy = lax.rem(y + k // pos.nx, pos.ny)
            pl.semaphore_signal(barrier, inc=1, device_id=pos.dev(xx, yy, z, c), device_id_type=MESH)
            return carry

        lax.fori_loop(1, pos.nx * pos.ny, body, 0)
        n += pos.nx * pos.ny - 1
    return n


def relay_kernel(pos, dims, refs):
    nx, ny, nz = pos.nx, pos.ny, pos.nz
    nxy = nx * ny
    parts, rows, piece, top = dims["parts"], dims["rows"], dims["piece"], dims["top"]
    depth, lane, tok, cap = dims["depth"], dims["lane"], dims["tok"], dims["cap"]
    feats = nz * piece
    half = nx * lane // 2
    (count_ref, tokens_ref, names_ref, prob_ref, wg_ref, wu_ref, wd_ref, final_ref) = refs[:8]
    (tok_ref, meta_ref, perm, columns, info_ref, back_ref, back_wide, mixed, home) = refs[8:17]
    (raw, out_tok, x_in, wbuf, part, land, hid, perm_back, out, result) = refs[17:27]
    (zsend, zrecv, loc, wsend, wrecv, fsend, frecv, tsend, trecv, rsend, rrecv, asend, arecv, bsem, hsem) = refs[27:]
    me = pos.here()
    x, y, z, c = me
    weights = (wg_ref, wu_ref, wd_ref)
    partner = pos.dev(x, y, z, 1 - c)

    def remote(src, dst, s, r, dev):
        return pltpu.make_async_remote_copy(src, dst, s, r, device_id=dev, device_id_type=MESH)

    def wait(ref, sem):
        pltpu.make_async_copy(ref, ref, sem).wait()

    barrier = pltpu.get_barrier_semaphore()
    partners = signal_all(pos, x, y, z, c, barrier, True, "all", True)

    nzl, nzh = pos.nzl, pos.nzh
    nseg = piece // depth
    block = nzl * depth
    lanes = lax.broadcasted_iota(jnp.int32, (1, nzl * piece), 1)
    inner = lax.rem(lanes, piece)
    source = (inner // depth) * block + (lanes // piece) * depth + lax.rem(inner, depth)
    ids = lax.broadcasted_iota(jnp.int32, (nseg * block, nzl * piece), 0)
    perm[...] = jnp.where(ids == source, 1.0, 0.0).astype(BF16)

    def blocks_of(zh):
        return [pl.ds((((seg // 2) * nzh + zh) * 2 + seg % 2) * block, block) for seg in range(nseg)]

    for zh in range(nzh):
        left = jnp.concatenate([tokens_ref[:, b] for b in blocks_of(zh)], axis=1)
        got = jnp.dot(left, perm[...], preferred_element_type=F32).astype(BF16)
        for zl in range(nzl):
            tok_ref[zh * nzl + zl] = got[:, zl * piece : (zl + 1) * piece]

    experts = nxy
    expert_ids = lax.broadcasted_iota(jnp.int32, (experts, tok), 0)
    live = lax.broadcasted_iota(jnp.int32, (experts, tok), 1) < count_ref[0]
    named = [(expert_ids == names_ref[s : s + 1, :]) & live for s in range(top)]
    either = jnp.where(functools.reduce(jnp.logical_or, named), 1.0, 0.0).astype(BF16)
    sooner = lax.broadcasted_iota(jnp.int32, (tok, tok), 0) < lax.broadcasted_iota(jnp.int32, (tok, tok), 1)
    rank = jnp.dot(either, jnp.where(sooner, 1.0, 0.0).astype(BF16), preferred_element_type=F32)
    meta_ref[...] = jnp.zeros_like(meta_ref)
    meta_ref[top : 2 * top, :] = prob_ref[...]
    for s in range(top):
        place = jnp.where(named[s], (expert_ids * cap).astype(F32) + rank + 1.0, 0.0)
        meta_ref[s : s + 1, :] = jnp.sum(place, axis=0, keepdims=True) - 1.0

    pl.semaphore_wait(barrier, partners)

    def far_first(i):
        return nz // 2 + (1 - 2 * lax.rem(i, 2)) * ((i + 1) // 2)

    def raw_send(i, carry):
        zz = lax.rem(z + far_first(i), nz)
        dev = pos.dev(x, y, zz, c)
        remote(tok_ref.at[zz], raw.at[z], zsend.at[0], zrecv.at[0], dev).start()
        remote(meta_ref, info_ref.at[z], zsend.at[1], zrecv.at[1], dev).start()
        return carry

    lax.fori_loop(0, nz - 1, raw_send, 0)
    own_raw = pltpu.make_async_copy(tok_ref.at[z], raw.at[z], loc.at[0])
    own_meta = pltpu.make_async_copy(meta_ref, info_ref.at[z], loc.at[1])
    own_raw.start()
    own_meta.start()

    def w_src(m, w, e):
        return weights[m].at[e, :, pl.ds(w * lane, lane)]

    def w_dst(m, w, xs, ys, cs):
        return wbuf.at[w, m, ys, cs, :, pl.ds(pl.multiple_of(xs * lane, lane), lane)]

    def w_start(w, mats):
        def body(k, carry):
            xx = lax.rem(x + lax.rem(k, nx) + 1, nx)
            yy = lax.rem(y + far_first(k // nx), ny)
            dev = pos.dev(xx, yy, z, c)
            for m in mats:
                remote(w_src(m, w, yy * nx + xx), w_dst(m, w, x, y, c), wsend.at[m], wrecv.at[m, w], dev).start()
            return carry

        lax.fori_loop(0, nxy - 1, body, 0)
        for m in mats:
            pltpu.make_async_copy(w_src(m, w, y * nx + x), w_dst(m, w, x, y, c), loc.at[2 + 3 * w + m]).start()

    def w_forward(w, mats):
        for m in mats:
            pltpu.make_async_copy(w_src(m, w, y * nx + x), w_dst(m, w, x, y, c), loc.at[2 + 3 * w + m]).wait()
            wait(weights[m].at[pl.ds(0, nxy - 1), :, pl.ds(w * lane, lane)], wrecv.at[m, w])
            block = wbuf.at[w, m, :, c]
            remote(block, block, fsend, frecv.at[m, w], partner).start()

    def w_ready(w, mats):
        for m in mats:
            wait(wbuf.at[w, m, :, 0], frecv.at[m, w])

    w_start(0, (0, 1))

    own_raw.wait()
    own_meta.wait()
    for i, ref in ((1, info_ref), (0, raw)):
        wait(ref.at[pl.ds(0, nz - 1)], zsend.at[i])
        wait(ref.at[pl.ds(0, nz - 1)], zrecv.at[i])
    count = nx * rows

    def dy_of(i):
        return lax.rem(6 * nz - 3 * (z + far_first(i)), nz)

    def dispatch(i):
        yy = lax.rem(y + dy_of(i), ny)
        ids = lax.broadcasted_iota(jnp.int32, (count, raw.shape[1]), 0).astype(F32)
        base = (yy * count).astype(F32)
        picks = []
        for zz in range(nz):
            hit = None
            for s in range(top):
                same = ids == (info_ref[zz, s : s + 1, :] * nz + (zz - base))
                hit = same if hit is None else hit | same
            picks.append(jnp.where(hit, 1.0, 0.0).astype(BF16))
        pick = jnp.concatenate(picks, axis=1)
        got = jnp.dot(pick, raw[...].reshape(nz * tok, piece), preferred_element_type=F32).astype(BF16)
        out_tok[pl.ds(yy * nx, nx)] = got.reshape(nx, rows, piece)

    def t_dst(xs, ys):
        return x_in.at[ys, :, pl.ds(pl.multiple_of(xs * piece, piece), piece)]

    def t_send(i):
        dy = dy_of(i)
        yy = lax.rem(y + dy, ny)
        for dx in range(nx):
            xx = lax.rem(x + dx, nx)
            away = remote(out_tok.at[yy * nx + xx], t_dst(x, y), tsend.at[i], trecv.at[dy], pos.dev(xx, yy, z, c))
            if dx:
                away.start()
            else:

                @pl.when(dy != 0)
                def _():
                    away.start()

                @pl.when(dy == 0)
                def _():
                    pltpu.make_async_copy(out_tok.at[y * nx + x], t_dst(x, y), loc.at[11]).start()

    def t_sent(i):
        dy = dy_of(i)

        @pl.when(dy == 0)
        def _():
            wait(out_tok.at[pl.ds(0, nx - 1)], tsend.at[i])

        @pl.when(dy != 0)
        def _():
            wait(out_tok.at[pl.ds(0, nx)], tsend.at[i])

    dispatch(0)

    def d_body(i, carry):
        dispatch(i)
        t_send(i - 1)
        return carry

    lax.fori_loop(1, 5, d_body, 0)

    def d_late(i, carry):
        dispatch(i)
        t_sent(i - 5)
        t_send(i - 1)
        return carry

    lax.fori_loop(5, ny, d_late, 0)
    for zz in range(nz):
        columns[zz] = jnp.transpose(info_ref[zz])
    lanes = lax.broadcasted_iota(jnp.int32, (1, nseg * block), 1)
    inner = lax.rem(lanes, block)
    source = (inner // depth) * piece + (lanes // block) * depth + lax.rem(inner, depth)
    ids = lax.broadcasted_iota(jnp.int32, (nzl * piece, nseg * block), 0)
    perm_back[...] = jnp.where(ids == source, 1.0, 0.0).astype(BF16)
    t_sent(3)
    t_send(ny - 1)
    w_forward(0, (0, 1))
    t_sent(4)
    t_sent(5)
    w_start(1, (0,))
    w_start(1, (1,))

    def token_wait(i):
        dy = dy_of(i)

        @pl.when(dy == 0)
        def _():
            pltpu.make_async_copy(out_tok.at[y * nx + x], t_dst(x, y), loc.at[11]).wait()
            wait(x_in.at[0, :, pl.ds(0, (nx - 1) * piece)], trecv.at[0])

        @pl.when(dy != 0)
        def _():
            wait(x_in.at[0], trecv.at[dy])

    def spot(h, m):
        return slice((2 * h + m) * half, (2 * h + m + 1) * half)

    def first_part(order):
        js = [lax.rem(3 * (z + far_first(i)) + y, nz) for i in order]
        left = jnp.concatenate([x_in[j] for j in js], axis=0) if len(js) > 1 else x_in[js[0]]
        for m in range(2):
            res = jnp.dot(left, wbuf[0, m].reshape(ny * 2 * depth, nx * lane), preferred_element_type=F32).astype(BF16)
            for i, j in enumerate(js):
                for h in range(2):
                    part[0, j, :, spot(h, m)] = res[i * rows : (i + 1) * rows, h * half : (h + 1) * half]

    def product(w, mats):
        wide = nx * lane
        for m in mats:
            right = wbuf[w, m].reshape(ny * 2 * depth, wide)

            def body(i, carry):
                left = x_in[pl.ds(i * (ny // 2), ny // 2)].reshape(ny // 2 * rows, nx * piece)
                res = jnp.dot(left, right, preferred_element_type=F32).astype(BF16)
                span = pl.ds(i * (ny // 2), ny // 2)
                for h in range(2):
                    part[w, span, :, spot(h, m)] = res[:, h * half : (h + 1) * half].reshape(ny // 2, rows, half)
                return carry

            lax.fori_loop(0, 2, body, 0)

    step = (1, nz - 1)
    near = (pos.dev(x, y, lax.rem(z + 1, nz), c), pos.dev(x, y, lax.rem(z + nz - 1, nz), c))
    far = nz // 2
    chains = [(d, h, far if h == d else far - 1) for h in range(2) for d in range(2)]
    wide = nx * lane

    mine_at = lax.rem(3 * z + y, nz)

    def at(d, k):
        return lax.rem(3 * (z + (k if d == 0 else -k)) + y + 2 * nz, nz)

    def rs_send(w, d, h, i, src):
        remote(src, land.at[w, d, h, i], rsend, rrecv.at[w, d, h, i], near[d]).start()

    def rs_start(w, hs=(0, 1)):
        for d, h, n in chains:
            if h in hs:
                rs_send(w, d, h, 0, part.at[w, at(d, n), :, pl.ds(h * wide, wide)])

    def rs_mid(w, i, hs=(0, 1)):
        ready = None
        for d, h, n in chains:
            if h in hs and i < n:
                slot = land.at[w, d, h, i - 1]
                wait(slot, rrecv.at[w, d, h, i - 1])
                mine = part[w, at(d, n - i), :, pl.ds(h * wide, wide)]
                slot[...] = (slot[...].astype(F32) + mine.astype(F32)).astype(BF16)
                if ready is not None:
                    rs_send(w, *ready)
                ready = (d, h, i, slot)
        if ready is not None:
            rs_send(w, *ready)

    def hid_half(w, j, h):
        return hid.at[w, j, :, pl.ds(h * half, half)]

    def ag_send(w, d, h, i, j):
        block = hid_half(w, j, h)
        remote(block, block, asend, arecv.at[w, d, h, i], near[d]).start()

    def rs_final(w, h):
        total = part[w, mine_at, :, pl.ds(h * wide, wide)].astype(F32)
        for d, hh, n in chains:
            if hh == h:
                slot = land.at[w, d, h, n - 1]
                wait(slot, rrecv.at[w, d, h, n - 1])
                total = total + slot[...].astype(F32)
        gate, up = total[:, :half], total[:, half:]
        hid[w, mine_at, :, h * half : (h + 1) * half] = (gate / (1.0 + jnp.exp(-gate)) * up).astype(BF16)

    def ag_start(w, h):
        for d, hh, n in chains:
            if hh == h:
                ag_send(w, d, h, 0, mine_at)

    def ag_mid(w, i, hs=(0, 1)):
        for d, h, n in chains:
            if h in hs and i <= n:
                j = at(d, -i)
                wait(hid_half(w, j, h), arecv.at[w, d, h, i - 1])
                if i < n:
                    ag_send(w, d, h, i, j)

    def o_src(xx, j):
        return out.at[j, :, pl.ds(pl.multiple_of(xx * piece, piece), piece)]

    def down(w, js):
        left = jnp.concatenate([hid[w, j] for j in js], axis=0) if len(js) > 1 else hid[w, js[0]]
        right = wbuf[w, 2].reshape(ny * 2 * depth, wide)
        return lax.dot_general(left, right, (((1,), (1,)), ((), ())), preferred_element_type=F32)

    def early_rows(js):
        return functools.reduce(jnp.add, [down(w, js) for w in range(parts - 1)])

    def finish_rows(js, early=None):
        res = (early_rows(js) if early is None else early) + down(parts - 1, js)
        for i, j in enumerate(js):
            out[j] = res[i * rows : (i + 1) * rows].astype(BF16)

    def send_rows(js):
        for j in js:
            for dx in range(nx):
                xx = lax.rem(x + dx, nx)
                away = remote(o_src(xx, j), back_ref.at[y * nx + x], bsem.at[0], bsem.at[1], pos.dev(xx, j, z, c))
                if dx:
                    away.start()
                else:

                    @pl.when(j != y)
                    def _():
                        away.start()

                    @pl.when(j == y)
                    def _():
                        pltpu.make_async_copy(o_src(x, y), back_ref.at[y * nx + x], bsem.at[2]).start()

    w_ready(0, (0, 1))
    token_wait(0)
    token_wait(1)
    token_wait(2)
    first_part([0])
    first_part([1, 2])
    rs_start(0)
    token_wait(3)
    token_wait(4)
    first_part([3, 4])
    rs_mid(0, 1)
    token_wait(5)
    token_wait(6)
    first_part([5, 6])
    token_wait(7)
    first_part([7])
    w_start(2, (0,))
    rs_mid(0, 2)
    w_start(2, (1,))
    w_forward(1, (0, 1))
    rs_mid(0, 3)
    w_ready(1, (0,))
    product(1, (0,))
    w_ready(1, (1,))
    product(1, (1,))
    rs_start(1)
    for h in range(2):
        rs_final(0, h)
        ag_start(0, h)
    w_forward(2, (0,))
    rs_mid(1, 1)
    w_forward(2, (1,))
    w_ready(2, (0,))
    product(2, (0,))
    w_ready(2, (1,))
    product(2, (1,))
    rs_start(2)
    rs_mid(1, 2)
    w_start(0, (2,))
    ag_mid(0, 1)
    rs_mid(2, 1)
    w_start(1, (2,))
    rs_mid(1, 3)
    w_start(2, (2,))
    rs_mid(2, 2)
    ag_mid(0, 2)
    rs_final(1, 0)
    rs_final(1, 1)
    rs_mid(2, 3)
    ag_start(1, 0)
    ag_start(1, 1)
    ag_mid(0, 3)
    w_forward(0, (2,))
    w_forward(1, (2,))
    for h in range(2):
        rs_final(2, h)
        ag_start(2, h)
    w_forward(2, (2,))
    ag_mid(0, 4)
    ag_mid(1, 1)
    for w in range(parts):
        w_ready(w, (2,))
    finish_rows([mine_at])
    send_rows([mine_at])
    ag_mid(2, 1)
    ag_mid(1, 2)
    finish_rows([at(0, 1), at(1, 1)])
    send_rows([at(0, 1), at(1, 1)])
    ag_mid(2, 2)
    ag_mid(1, 3)
    finish_rows([at(0, 2), at(1, 2)])
    send_rows([at(0, 2), at(1, 2)])
    early = early_rows([at(0, 3), at(1, 3)])
    ag_mid(2, 3)
    ag_mid(1, 4)
    finish_rows([at(0, 3), at(1, 3)], early)
    send_rows([at(0, 3), at(1, 3)])
    early = early_rows([at(0, 4)])
    ag_mid(2, 4)
    finish_rows([at(0, 4)], early)
    send_rows([at(0, 4)])

    pltpu.make_async_copy(o_src(x, y), back_ref.at[y * nx + x], bsem.at[2]).wait()
    wait(back_ref.at[pl.ds(0, nxy - 1)], bsem.at[1])
    back_wide[...] = back_ref[...].reshape(nxy * rows, piece).astype(F32)
    slots = experts * cap
    slot_ids = lax.broadcasted_iota(jnp.int32, (tok, slots), 1).astype(F32)

    def combine(i):
        zz = lax.rem(z + far_first(i), nz)
        mine = back_wide[pl.ds(zz, slots, stride=nz), :].astype(BF16)
        cols = columns[zz]
        total = jnp.zeros((tok, piece), F32)
        for s in range(top):
            chosen = jnp.where(slot_ids == cols[:, s : s + 1], 1.0, 0.0).astype(BF16)
            total = total + cols[:, top + s : top + s + 1] * jnp.dot(chosen, mine, preferred_element_type=F32)
        mixed[zz] = total.astype(BF16)

    def home_send(i):
        zz = lax.rem(z + far_first(i), nz)
        remote(mixed.at[zz], home.at[z], hsem.at[0], hsem.at[1], pos.dev(x, y, zz, c)).start()

    combine(0)

    def home_body(i, carry):
        combine(i)
        home_send(i - 1)
        return carry

    lax.fori_loop(1, nz, home_body, 0)
    own_home = pltpu.make_async_copy(mixed.at[z], home.at[z], hsem.at[2])
    own_home.start()

    for m in range(3):
        wait(weights[m].at[pl.ds(0, nxy - 1)], wsend.at[m])
    wait(wbuf.at[:, :, :, 0], fsend)
    wait(part.at[:, pl.ds(0, nz - 1)], rsend)
    wait(hid.at[:, pl.ds(0, nz - 1)], asend)
    for i in (ny - 2, ny - 1):
        t_sent(i)
    wait(back_ref.at[pl.ds(0, nxy - 1)], bsem.at[0])
    own_home.wait()
    wait(mixed.at[pl.ds(0, nz - 1)], hsem.at[0])
    wait(home.at[pl.ds(0, nz - 1)], hsem.at[1])
    for zh in range(nzh):
        left = jnp.concatenate([home[zh * nzl + zl] for zl in range(nzl)], axis=1)
        got = jnp.dot(left, perm_back[...], preferred_element_type=F32).astype(BF16)
        for seg, b in enumerate(blocks_of(zh)):
            result[:, b] = got[:, seg * block : (seg + 1) * block]
    leave = pltpu.make_async_copy(result, final_ref, hsem.at[2])
    leave.start()
    leave.wait()


def relay(pos, cid, token_count, tokens, names, probs, w_gate, w_up, w_down, cap):
    nx, ny, nz = pos.nx, pos.ny, pos.nz
    nxy = nx * ny
    _, depth, width = w_gate.shape
    tok, feats = tokens.shape
    piece = feats // nz
    lane = 128
    parts = width // lane
    rows = nz * cap
    wide = nx * lane
    dims = {
        "parts": parts, "rows": rows, "piece": piece, "top": 2, "depth": depth, "lane": lane, "tok": tok, "cap": cap
    }
    any_spec = pl.BlockSpec(memory_space=pl.ANY)
    vmem = pl.BlockSpec(memory_space=pltpu.VMEM)
    smem = pl.BlockSpec(memory_space=pltpu.SMEM)
    dma = pltpu.SemaphoreType.DMA
    return pl.pallas_call(
        lambda *refs: relay_kernel(pos, dims, refs),
        out_shape=jax.ShapeDtypeStruct((tok, feats), BF16),
        in_specs=[smem, vmem, vmem, vmem, any_spec, any_spec, any_spec],
        out_specs=any_spec,
        scratch_shapes=[
            pltpu.VMEM((nz, tok, piece), BF16),
            pltpu.VMEM((8, tok), F32),
            pltpu.VMEM((feats // 2, feats // 2), BF16),
            pltpu.VMEM((nz, tok, 8), F32),
            pltpu.VMEM((nz, 8, tok), F32),
            pltpu.VMEM((nxy, rows, piece), BF16),
            pltpu.VMEM((nxy * rows, piece), F32),
            pltpu.VMEM((nz, tok, piece), BF16),
            pltpu.VMEM((nz, tok, piece), BF16),
            pltpu.VMEM((nz, tok, piece), BF16),
            pltpu.VMEM((nxy, rows, piece), BF16),
            pltpu.VMEM((ny, rows, nx * piece), BF16),
            pltpu.VMEM((parts, 3, ny, 2, depth, wide), BF16),
            pltpu.VMEM((parts, nz, rows, 2 * wide), BF16),
            pltpu.VMEM((parts, 2, 2, nz // 2, rows, wide), BF16),
            pltpu.VMEM((parts, nz, rows, wide), BF16),
            pltpu.VMEM((feats // 2, feats // 2), BF16),
            pltpu.VMEM((nz, rows, nx * piece), BF16),
            pltpu.VMEM((tok, feats), BF16),
            dma((2,)),
            dma((2,)),
            dma((12,)),
            dma((3,)),
            dma((3, parts)),
            dma,
            dma((3, parts)),
            dma((ny,)),
            dma((ny,)),
            dma,
            dma((parts, 2, 2, nz // 2)),
            dma,
            dma((parts, 2, 2, nz // 2)),
            dma((3,)),
            dma((3,)),
        ],
        compiler_params=pltpu.CompilerParams(
            collective_id=cid, has_side_effects=True, vmem_limit_bytes=56 * 1024 * 1024
        ),
        name="relay",
    )(token_count, tokens, names, probs, w_gate, w_up, w_down)


def shards(pos, tokens, routes, gate_prob, token_count, gate_weight, up_weight, down_weight):
    experts = gate_weight.shape[0]
    tok, top = routes.shape
    cap = min(tok, tok * top * 5 // (4 * experts))
    return relay(pos, 1, token_count, tokens, routes.T, gate_prob.T, gate_weight, up_weight, down_weight, cap)


def solution(mesh):
    nzl = mesh.shape["dp"]
    nx = mesh.shape["tensor"]
    nzh = 2
    ny = mesh.shape["expert"] // (2 * nzh)
    pos = Place(nx, ny, nzh * nzl, nzl)
    in_specs = (
        P(("expert", "dp"), "tensor"),
        P(("expert", "dp"), None),
        P(("expert", "dp"), None),
        P(("expert", "dp")),
        P(None, ("expert", "dp"), "tensor"),
        P(None, ("expert", "dp"), "tensor"),
        P(None, ("expert", "dp"), "tensor"),
    )
    out_specs = P(("expert", "dp"), "tensor")
    return jax.shard_map(
        functools.partial(shards, pos), mesh=mesh, in_specs=in_specs, out_specs=out_specs, check_vma=False
    )
```
